512 devices in a mesh: tx: 8 (over y, core), ty: 8 (over x, z_hi), ang: 8 (over z_lo).
Axes of the slice: x: 4, y: 4, z: 16 (z_hi: 2, z_lo: 8; z = z_hi * 8 + z_lo), core: 2. Of those that a mesh axis runs over, the one named last changes fastest.
Arguments:
- projections: bfloat16 [8, 8, 128, 8, 1024], P('tx', 'ty', 'ang'), may hold values from -6 to 6
- view_angles: float32 [8, 8, 128], P('tx', 'ty', 'ang'), may hold values from -3.140625 to 3.140625
- tilt: float32 [8, 8], P('tx', 'ty'), may hold values from 0.3 to 0.7
- offsets: int32 [8, 8], P('tx', 'ty'), may hold values from 0 to 128
- extents: int32 [8, 8], P('tx', 'ty'), may hold values from 1 to 4
- feather: int32 [8, 8, 2, 4], P('tx', 'ty'), may hold values from 0 to 8
Outputs:
- seams: float32 [8, 8, 8, 4, 1024], P('tx', 'ty', 'ang')
- lower_bands: float32 [8, 8, 8, 4, 1024], P('tx', 'ty', 'ang')
The draws below stay inside these ranges and needn't reach their ends.
All inputs are finite; a program needn't handle non-finite values.
Results may differ from the reference program's by a relative error of at most 0.0028.
Values sent between devices are 32-bit elements; how exact they have to be, the bound alone decides.
A program may use at most 64 MiB of HBM per device.

```python
import math
import jax
import jax.numpy as jnp
from jax import lax

U = 1024
B = 4
DXMAX = 128
NZ = 8
VIEWS = 128
TILES_X = 8
TILES_Y = 8
ROWS = 8


def plant(values, key, least, largest):
    spot = [jax.random.randint(jax.random.fold_in(key, axis), (), 0, length) for axis, length in enumerate(values.shape)]
    longest = values.shape.index(max(values.shape))
    neighbour = spot[:longest] + [(spot[longest] + 1) % values.shape[longest]] + spot[longest + 1:]
    return values.at[tuple(spot)].set(least).at[tuple(neighbour)].set(largest)


def levels(key, dims, split, smallest, top_value):
    loudness = 1.0
    for position, shards_of in split:
        draws = jax.random.uniform(jax.random.fold_in(jax.random.fold_in(key, 6), position), (shards_of,), jnp.float32, smallest / len(split), top_value / len(split))
        loudness = loudness * jnp.repeat(jnp.exp(draws), dims[position] // shards_of).reshape((-1,) + (1,) * (len(dims) - 1 - position))
    return loudness


def centred(own_key, dims, scale, limit, split=(), kind=jnp.bfloat16):
    level = levels(own_key, dims, split, -0.22, 0.18) if split else 1.0
    entries = jax.random.normal(own_key, dims, jnp.float32) * scale * level
    return jnp.minimum(jnp.maximum(entries, -limit), limit).astype(kind)


def setup_inputs(seed: int = 0) -> dict:
    arg_keys = jax.random.split(jax.random.key(seed), 7)
    projections = centred(arg_keys[0], (TILES_X, TILES_Y, VIEWS, ROWS, U), 1.0, 6.0, ((0, 8), (1, 8), (2, 8)))
    view_angles = jnp.clip(jax.random.uniform(arg_keys[1], (TILES_X, TILES_Y, VIEWS), jnp.float32, -3.140625, 3.140625), -3.140625, 3.140625)
    tilt = jnp.clip(0.3 + 0.39999998 * jax.random.uniform(arg_keys[2], (TILES_X, TILES_Y), jnp.float32) ** levels(arg_keys[2], (TILES_X, TILES_Y), ((0, 8), (1, 8)), -0.2, 0.2), 0.3, 0.7)
    offsets = plant(jax.random.randint(arg_keys[3], (TILES_X, TILES_Y), 0, DXMAX + 1), jax.random.fold_in(arg_keys[3], 1), 0, DXMAX).astype(jnp.int32)
    extents = plant(jax.random.randint(arg_keys[4], (TILES_X, TILES_Y), 1, B + 1), jax.random.fold_in(arg_keys[4], 1), 1, B).astype(jnp.int32)
    feather = plant(jax.random.randint(arg_keys[5], (TILES_X, TILES_Y, 2, B), 0, 9), jax.random.fold_in(arg_keys[5], 1), 0, 8).astype(jnp.int32)
    return dict(projections=projections, view_angles=view_angles, tilt=tilt, offsets=offsets, extents=extents, feather=feather)


PITCH = 16.0

def forward_table(width, start, count):
    column = jnp.arange(width, dtype=jnp.int32)[:, None]
    freq = start + jnp.arange(count, dtype=jnp.int32)[None, :]
    turn = (column * freq % width).astype(jnp.float32) * (2.0 * math.pi / width)
    filt = (freq.astype(jnp.float32) + 0.5) / (width // 2) / math.sqrt(width)
    return jnp.concatenate([jnp.cos(turn) * filt, -jnp.sin(turn) * filt], axis=1).astype(jnp.bfloat16)

def phase_pair(shift, width, start, count):
    freq = (start + jnp.arange(count, dtype=jnp.int32)).astype(jnp.float32)
    turn = shift[..., None] * freq * (2.0 * math.pi / width)
    return (jnp.cos(turn), jnp.sin(turn))

def fourier_sum(proj, angles, lean, planes, width):
    views, rows, _ = proj.shape
    half = width // 2
    block = min(128, half)
    band = rows // 2
    flat = proj.reshape(views * rows, width)
    ycoord = jnp.concatenate([jnp.arange(band, dtype=jnp.int32), width - band + jnp.arange(band, dtype=jnp.int32)]).astype(jnp.float32) - width / 2
    zcoord = (jnp.arange(planes, dtype=jnp.int32).astype(jnp.float32) - (planes - 1) / 2) * PITCH
    zshift = lean * jnp.cos(angles)[:, None] * zcoord[None, :]
    yshift = lean * jnp.sin(angles)[:, None] * ycoord[None, :]

    def one_block(index):
        start = index * block
        table = forward_table(width, start, block)
        spec = jnp.dot(flat, table, preferred_element_type=jnp.float32).reshape(views, rows, 2 * block)
        spec_re = spec[..., :block]
        spec_im = spec[..., block:]
        ycos, ysin = phase_pair(yshift, width, start, block)
        prod_re = spec_re * ycos - spec_im * ysin
        prod_im = spec_re * ysin + spec_im * ycos
        zcos, zsin = phase_pair(zshift, width, start, block)
        high = lax.Precision.HIGHEST
        real = jnp.einsum('kzf,kyf->zyf', zcos, prod_re, precision=high) - jnp.einsum('kzf,kyf->zyf', zsin, prod_im, precision=high)
        imag = jnp.einsum('kzf,kyf->zyf', zcos, prod_im, precision=high) + jnp.einsum('kzf,kyf->zyf', zsin, prod_re, precision=high)
        return (real, imag)
    real, imag = lax.map(one_block, jnp.arange(half // block, dtype=jnp.int32))
    real = jnp.moveaxis(real, 0, 2).reshape(planes, rows, half)
    imag = jnp.moveaxis(imag, 0, 2).reshape(planes, rows, half)
    return (real, imag)

def to_image(real, imag, width):
    half = width // 2
    cols = min(512, width)
    lead = real.shape[:-1]
    left = jnp.concatenate([real, imag], axis=-1).reshape(-1, width)

    def one_block(index):
        freq = jnp.arange(half, dtype=jnp.int32)[:, None]
        place = index * cols + jnp.arange(cols, dtype=jnp.int32)[None, :]
        turn = (freq * place % width).astype(jnp.float32) * (2.0 * math.pi / width)
        table = jnp.concatenate([jnp.cos(turn), -jnp.sin(turn)], axis=0) * math.sqrt(2.0 / width)
        return jnp.dot(left, table, precision=lax.Precision.HIGHEST, preferred_element_type=jnp.float32)
    out = lax.map(one_block, jnp.arange(width // cols, dtype=jnp.int32))
    return jnp.moveaxis(out, 0, 1).reshape(lead + (width,))

def reference(projections, view_angles, tilt, offsets, extents, feather):
    tiles_x = projections.shape[0]
    tiles_y = projections.shape[1]
    flat_proj = projections.reshape((tiles_x * tiles_y,) + projections.shape[2:])

    def one_tile(items):
        proj, angles, lean = items
        real, imag = fourier_sum(proj, angles, lean, NZ, U)
        scale = 1.0 / math.sqrt(VIEWS)
        return to_image(real * scale, imag * scale, U)
    image = lax.map(one_tile, (flat_proj, view_angles.reshape(-1, VIEWS), tilt.reshape(-1)))
    image = image.reshape(tiles_x, tiles_y, NZ, 2 * B, U)
    top = image[:, :, :, :B]
    bottom = image[:, :, :, B:]
    below = jnp.concatenate([jnp.zeros_like(bottom[:, :1]), bottom[:, :-1]], axis=1)
    corner = jnp.concatenate([below[1:, :, :, :, :DXMAX], jnp.zeros_like(below[:1, :, :, :, :DXMAX])], axis=0)
    joined = jnp.concatenate([below, corner], axis=-1)

    def take(piece, start):
        return lax.dynamic_slice_in_dim(piece, start.astype(jnp.int32), U, 2)
    aligned = jax.vmap(jax.vmap(take))(joined, offsets)
    row = jnp.arange(B, dtype=jnp.int32)
    upper = (jnp.arange(tiles_y, dtype=jnp.int32) > 0).astype(jnp.float32)
    own = feather[:, :, 0, :].astype(jnp.float32)
    other = feather[:, :, 1, :].astype(jnp.float32) * (row[None, None, :] < extents[:, :, None]).astype(jnp.float32) * upper[None, :, None]
    total = jnp.maximum(own + other, 1.0)
    seams = (own[:, :, None, :, None] * top + other[:, :, None, :, None] * aligned) / total[:, :, None, :, None]
    return (seams, bottom)
```

```python
import functools
import math

import jax
import jax.numpy as jnp
import ml_dtypes
import numpy as np
from jax import lax
from jax.experimental import pallas as pl
from jax.experimental.pallas import tpu as pltpu
from jax.sharding import PartitionSpec as P

MESH = pl.DeviceIdType.MESH
PITCH = 16.0
U = 1024
F = U // 2
BLOCK = 128
DXMAX = 128

SIN_HALF = (3.1415926401307073, -5.167710083507923, 2.5500775232148563, -0.5982912856211671, 0.07765766030589402)
COS_HALF = (0.9999999532476085, -4.934792830619664, 4.058411352862771, -1.3318765680813944, 0.21968961109803095)


def frequency_order():
    return np.concatenate([np.arange(0, F, 2), np.arange(1, F, 2)])


def forward_half_table():
    freq = frequency_order()[None, :]
    column = np.arange(U // 2)[:, None]
    turn = (column * freq % U) * (2.0 * math.pi / U)
    filt = (freq + 0.5) / F / math.sqrt(U)
    both = np.concatenate([np.cos(turn) * filt, -np.sin(turn) * filt], axis=1)
    return both.astype(np.float32).astype(ml_dtypes.bfloat16)


def inverse_half_tables(views):
    scale = math.sqrt(2.0 / U) / math.sqrt(views)
    place = np.arange(U // 2)[None, :]
    halves = []
    for start in (0, 1):
        freq = np.arange(start, F, 2)[:, None]
        turn = (freq * place % U) * (2.0 * math.pi / U)
        halves.append(np.concatenate([np.cos(turn), -np.sin(turn)], axis=0) * scale)
    return np.stack(halves).astype(np.float32).astype(ml_dtypes.bfloat16)


def horner(z, coefficients):
    total = jnp.full_like(z, coefficients[-1])
    for c in coefficients[-2::-1]:
        total = total * z + c
    return total


def cos_sin_turns(t):
    r = t - jnp.round(t)
    z = r * r
    s = r * horner(z, SIN_HALF)
    c = horner(z, COS_HALF)
    return 1.0 - 2.0 * (s * s), 2.0 * (s * c)


def cos_sin_angle(theta):
    h = theta * 0.5
    z = h * h
    s = h * horner(z, [(-1.0) ** n / math.factorial(2 * n + 1) for n in range(8)])
    c = horner(z, [(-1.0) ** n / math.factorial(2 * n) for n in range(9)])
    return 1.0 - 2.0 * (s * s), 2.0 * (s * c)


def kernel(
    sizes, views,
    x_hbm, g_hbm, t_hbm, angles_ref, tilt_ref, offset_ref, extent_ref, feather_ref,
    seams_ref, lower_ref,
    x_buf, g_buf, t_buf, spec_buf, ycos, ysin, zcos, zsin, col_buf, q_buf,
    bot, top, bot_in, top_in, bot_sum, below_in, corner_in,
    load_sem, send_sem, recv_sem,
):
    n_tx, n_ty, n_ang = sizes
    tx, ty, me = lax.axis_index("tx"), lax.axis_index("ty"), lax.axis_index("ang")
    ty_prev, ty_next = lax.rem(ty + n_ty - 1, n_ty), lax.rem(ty + 1, n_ty)
    tx_prev, tx_next = lax.rem(tx + n_tx - 1, n_tx), lax.rem(tx + 1, n_tx)

    barrier = pltpu.get_barrier_semaphore()
    for d in range(1, n_ang):
        peer = lax.rem(me + d, n_ang)
        pl.semaphore_signal(barrier, inc=1, device_id=(tx, ty, peer), device_id_type=MESH)
    pl.semaphore_signal(barrier, inc=1, device_id=(tx, ty_prev, me), device_id_type=MESH)
    pl.semaphore_signal(barrier, inc=1, device_id=(tx_next, ty_prev, me), device_id_type=MESH)

    load_x = pltpu.make_async_copy(x_hbm, x_buf, load_sem.at[0])
    load_g = pltpu.make_async_copy(g_hbm, g_buf, load_sem.at[1])
    load_t = pltpu.make_async_copy(t_hbm, t_buf, load_sem.at[2])
    load_x.start()
    load_g.start()
    load_t.start()

    lean = tilt_ref[0, 0]
    rows_i = lax.broadcasted_iota(jnp.int32, (views, views), 0)
    cols_i = lax.broadcasted_iota(jnp.int32, (views, views), 1)
    spread = jnp.where(rows_i == cols_i, jnp.broadcast_to(angles_ref[...], (views, views)), 0.0)
    theta = jnp.broadcast_to(jnp.sum(spread, axis=1, keepdims=True), (views, BLOCK))
    cth, sth = cos_sin_angle(theta)
    col_buf[...] = sth * lean
    zcoef = cth * (lean * (0.5 * PITCH / U))
    band = 4
    sub = lax.broadcasted_iota(jnp.int32, (8, BLOCK), 0)
    ycoord = jnp.where(sub < band, sub, sub + (U - 2 * band)) - U // 2
    ycoef = ycoord.astype(jnp.float32) * (1.0 / U)
    lane = lax.broadcasted_iota(jnp.int32, (8, BLOCK), 1)
    for i in range(4):
        at = slice(BLOCK * i, BLOCK * (i + 1))
        freq8 = (lane * 2 + (2 * BLOCK * (i % 2) + i // 2)).astype(jnp.float32)
        freq = jnp.concatenate([freq8] * (views // 8), axis=0)
        c1, s1 = cos_sin_turns(zcoef * freq)
        c2, s2 = 1.0 - 2.0 * (s1 * s1), 2.0 * (s1 * c1)
        c, s = c1, s1
        for j in range(4):
            zcos[j, :, at] = c
            zsin[j, :, at] = s
            if j < 3:
                c, s = c * c2 - s * s2, c * s2 + s * c2
        for k in range(views):
            slope = jnp.broadcast_to(col_buf[k : k + 1, :], (8, BLOCK)) * ycoef
            c, s = cos_sin_turns(slope * freq8)
            ycos[8 * k : 8 * k + 8, at] = c
            ysin[8 * k : 8 * k + 8, at] = s

    load_x.wait()
    load_g.wait()
    rows = views * 8
    left = x_buf[:, :, : U // 2].reshape(rows, U // 2)
    right = x_buf[:, :, U // 2 :].reshape(rows, U // 2)
    spec_buf[...] = jnp.dot(
        jnp.concatenate([left, right], axis=0), g_buf[...], preferred_element_type=jnp.float32
    )

    for i in range(4):
        at = slice(BLOCK * i, BLOCK * (i + 1))
        at_im = slice(F + BLOCK * i, F + BLOCK * (i + 1))
        acc = [[jnp.zeros((8, BLOCK), jnp.float32) for _ in range(4)] for _ in range(4)]
        for k in range(views):
            here, there = slice(8 * k, 8 * k + 8), slice(rows + 8 * k, rows + 8 * k + 8)
            if i < 2:
                s_re = spec_buf[here, at] + spec_buf[there, at]
                s_im = spec_buf[here, at_im] + spec_buf[there, at_im]
            else:
                s_re = spec_buf[here, at] - spec_buf[there, at]
                s_im = spec_buf[here, at_im] - spec_buf[there, at_im]
            yc, ys = ycos[here, at], ysin[here, at]
            p_re = s_re * yc - s_im * ys
            p_im = s_re * ys + s_im * yc
            for j in range(4):
                c = jnp.broadcast_to(zcos[j, k : k + 1, at], (8, BLOCK))
                s = jnp.broadcast_to(zsin[j, k : k + 1, at], (8, BLOCK))
                acc[j][0] += c * p_re
                acc[j][1] += c * p_im
                acc[j][2] += s * p_re
                acc[j][3] += s * p_im
        part, col = i // 2, BLOCK * (i % 2)
        for j in range(4):
            c_re, c_im, s_re, s_im = acc[j]
            for plane, re, im in (
                (4 + j, c_re - s_im, c_im + s_re),
                (3 - j, c_re + s_im, c_im - s_re),
            ):
                at_row = slice(8 * plane, 8 * plane + 8)
                q_buf[part, at_row, col : col + BLOCK] = re
                q_buf[part, at_row, F // 2 + col : F // 2 + col + BLOCK] = im

    load_t.wait()
    halves = []
    for part in range(2):
        q = q_buf[part]
        high = q.astype(jnp.bfloat16)
        low = (q - high.astype(jnp.float32)).astype(jnp.bfloat16)
        both = jnp.dot(
            jnp.concatenate([high, low], axis=0), t_buf[part], preferred_element_type=jnp.float32
        )
        halves.append(both[: 8 * 8] + both[8 * 8 :])
    first, second = halves[0] + halves[1], halves[0] - halves[1]
    sub_wide = lax.broadcasted_iota(jnp.int32, (8, F), 0)
    upper = sub_wide < band
    for plane in range(8):
        a, b = first[8 * plane : 8 * plane + 8], second[8 * plane : 8 * plane + 8]
        bot[plane] = jnp.where(upper, pltpu.roll(a, band, 0), b)
        top[plane] = jnp.where(upper, a, pltpu.roll(b, band, 0))

    pl.semaphore_wait(barrier, n_ang + 1)

    order = sorted(range(1, n_ang), key=lambda d: abs(d - n_ang // 2))
    copies = []
    for which, (src, dst) in enumerate(((bot, bot_in), (top, top_in))):
        group = []
        for d in order:
            peer = lax.rem(me + d, n_ang)
            copy = pltpu.make_async_remote_copy(
                src_ref=src.at[peer], dst_ref=dst.at[d - 1],
                send_sem=send_sem.at[which * n_ang + d], recv_sem=recv_sem.at[which * n_ang + d],
                device_id=(tx, ty, peer), device_id_type=MESH,
            )
            copy.start()
            group.append(copy)
        copies.append(group)

    def gathered(which, mine, landed):
        total = mine[me]
        for d, copy in zip(order, copies[which]):
            copy.wait_recv()
            total += landed[d - 1]
        return total

    bottom = gathered(0, bot, bot_in)
    bot_sum[...] = bottom
    down = pltpu.make_async_remote_copy(
        src_ref=bot_sum, dst_ref=below_in, send_sem=send_sem.at[0], recv_sem=recv_sem.at[0],
        device_id=(tx, ty_next, me), device_id_type=MESH,
    )
    across = pltpu.make_async_remote_copy(
        src_ref=bot_sum.at[:, pl.ds(0, BLOCK)], dst_ref=corner_in,
        send_sem=send_sem.at[n_ang], recv_sem=recv_sem.at[n_ang],
        device_id=(tx_prev, ty_next, me), device_id_type=MESH,
    )
    across.start()
    down.start()

    lower_ref[:, :F] = bottom[:band]
    lower_ref[:, F:] = pltpu.roll(bottom, band, 0)[:band]
    own_top = gathered(1, top, top_in)

    row = sub % band
    own = jnp.zeros((8, BLOCK), jnp.float32)
    other = jnp.zeros((8, BLOCK), jnp.float32)
    seen = (ty > 0).astype(jnp.int32)
    for r in range(band):
        a = feather_ref[0, 0, r].astype(jnp.float32)
        b = (feather_ref[0, 1, r] * (r < extent_ref[0, 0]).astype(jnp.int32) * seen).astype(jnp.float32)
        own = jnp.where(row == r, a, own)
        other = jnp.where(row == r, b, other)
    total = jnp.maximum(own + other, 1.0)
    own, other = own / total, other / total
    shift = offset_ref[0, 0]
    turn_by = (BLOCK - shift) & (BLOCK - 1)

    across.wait_recv()
    down.wait_recv()
    below = below_in[...]
    corner = jnp.where(tx < n_tx - 1, corner_in[...], 0.0)
    tail = pltpu.roll(jnp.where(sub < band, corner, below[:, :BLOCK]), band, 0)
    pieces = [below[:, BLOCK * i : BLOCK * (i + 1)] for i in range(4)] + [tail]
    turned = [pltpu.roll(piece, turn_by, 1) for piece in pieces]
    for i in range(4):
        aligned = jnp.where(lane < BLOCK - shift, turned[i], turned[i + 1])
        seam = own * own_top[:, BLOCK * i : BLOCK * (i + 1)] + other * aligned
        seams_ref[:, BLOCK * i : BLOCK * (i + 1)] = seam[:band]
        seams_ref[:, F + BLOCK * i : F + BLOCK * (i + 1)] = pltpu.roll(seam, band, 0)[:band]

    for group in copies:
        for copy in group:
            copy.wait_send()
    across.wait_send()
    down.wait_send()


def solution(mesh):
    sizes = tuple(mesh.shape[name] for name in ("tx", "ty", "ang"))
    n_ang = sizes[2]

    def on_device(projections, view_angles, tilt, offsets, extents, feather):
        _, _, views, rows, width = projections.shape
        band = rows // 2
        g = jnp.asarray(forward_half_table())
        t = jnp.asarray(inverse_half_tables(views * n_ang))
        smem = pl.BlockSpec(memory_space=pltpu.SMEM)
        vmem = pl.BlockSpec(memory_space=pltpu.VMEM)
        hbm = pl.BlockSpec(memory_space=pl.ANY)
        f32 = jnp.float32
        seams, lower = pl.pallas_call(
            functools.partial(kernel, sizes, views),
            out_shape=[jax.ShapeDtypeStruct((band, width), f32)] * 2,
            in_specs=[hbm, hbm, hbm, vmem, smem, smem, smem, smem],
            out_specs=[vmem, vmem],
            scratch_shapes=[
                pltpu.VMEM((views, rows, width), jnp.bfloat16),
                pltpu.VMEM((F, width), jnp.bfloat16),
                pltpu.VMEM((2, F, F), jnp.bfloat16),
                pltpu.VMEM((2 * views * rows, width), f32),
                pltpu.VMEM((views * rows, F), f32),
                pltpu.VMEM((views * rows, F), f32),
                pltpu.VMEM((4, views, F), f32),
                pltpu.VMEM((4, views, F), f32),
                pltpu.VMEM((views, BLOCK), f32),
                pltpu.VMEM((2, n_ang * rows, F), f32),
                pltpu.VMEM((n_ang, rows, F), f32),
                pltpu.VMEM((n_ang, rows, F), f32),
                pltpu.VMEM((n_ang - 1, rows, F), f32),
                pltpu.VMEM((n_ang - 1, rows, F), f32),
                pltpu.VMEM((rows, F), f32),
                pltpu.VMEM((rows, F), f32),
                pltpu.VMEM((rows, BLOCK), f32),
                pltpu.SemaphoreType.DMA((3,)),
                pltpu.SemaphoreType.DMA((2 * n_ang,)),
                pltpu.SemaphoreType.DMA((2 * n_ang,)),
            ],
            compiler_params=pltpu.CompilerParams(collective_id=0, has_side_effects=True),
        )(projections[0, 0], g, t, view_angles[0], tilt, offsets, extents, feather[0])
        return (seams[None, None, None], lower[None, None, None])

    in_specs = (
        P("tx", "ty", "ang", None, None),
        P("tx", "ty", "ang"),
        P("tx", "ty"),
        P("tx", "ty"),
        P("tx", "ty"),
        P("tx", "ty", None, None),
    )
    out_specs = (P("tx", "ty", "ang", None, None), P("tx", "ty", "ang", None, None))
    return jax.shard_map(
        on_device, mesh=mesh, in_specs=in_specs, out_specs=out_specs, check_vma=False
    )
```

```python
import functools
import math

import jax
import jax.numpy as jnp
import ml_dtypes
import numpy as np
from jax import lax
from jax.experimental import pallas as pl
from jax.experimental.pallas import tpu as pltpu
from jax.sharding import PartitionSpec as P

MESH = pl.DeviceIdType.MESH
PITCH = 16.0
U = 1024
F = U // 2
BLOCK = 128
DXMAX = 128

SIN_HALF = (3.1415926401307073, -5.167710083507923, 2.5500775232148563, -0.5982912856211671, 0.07765766030589402)
COS_HALF = (0.9999999532476085, -4.934792830619664, 4.058411352862771, -1.3318765680813944, 0.21968961109803095)


def frequency_order():
    return np.concatenate([np.arange(0, F, 2), np.arange(1, F, 2)])


def forward_half_table():
    freq = frequency_order()[None, :]
    column = np.arange(U // 2)[:, None]
    turn = (column * freq % U) * (2.0 * math.pi / U)
    filt = (freq + 0.5) / F / math.sqrt(U)
    both = np.concatenate([np.cos(turn) * filt, -np.sin(turn) * filt], axis=1)
    return both.astype(np.float32).astype(ml_dtypes.bfloat16)


def inverse_half_tables(views):
    scale = math.sqrt(2.0 / U) / math.sqrt(views)
    place = np.arange(U // 2)[None, :]
    halves = []
    for start in (0, 1):
        freq = np.arange(start, F, 2)[:, None]
        turn = (freq * place % U) * (2.0 * math.pi / U)
        halves.append(np.concatenate([np.cos(turn), -np.sin(turn)], axis=0) * scale)
    return np.stack(halves).astype(np.float32).astype(ml_dtypes.bfloat16)


def horner(z, coefficients):
    total = jnp.full_like(z, coefficients[-1])
    for c in coefficients[-2::-1]:
        total = total * z + c
    return total


def cos_sin_turns(t):
    r = t - jnp.round(t)
    z = r * r
    s = r * horner(z, SIN_HALF)
    c = horner(z, COS_HALF)
    return 1.0 - 2.0 * (s * s), 2.0 * (s * c)


def cos_sin_angle(theta):
    h = theta * 0.5
    z = h * h
    s = h * horner(z, [(-1.0) ** n / math.factorial(2 * n + 1) for n in range(8)])
    c = horner(z, [(-1.0) ** n / math.factorial(2 * n) for n in range(9)])
    return 1.0 - 2.0 * (s * s), 2.0 * (s * c)


def kernel(
    sizes, views,
    x_hbm, g_hbm, t_hbm, angles_hbm, tilt_hbm, offset_hbm, extent_hbm, feather_hbm,
    seams_ref, lower_ref,
    angles_ref, tilt_ref, offset_ref, extent_ref, feather_ref, x_buf, g_buf, t_buf, spec_buf, ycos, ysin, zcos, zsin, col_buf, q_buf,
    bot, top, bot_in, top_in, bot_sum, top_sum, cross_in, below_buf, corner_in,
    load_sem, small_sem, send_sem, recv_sem, ready_sem,
):
    n_tx, n_ty, n_ang = sizes
    tx, ty, me = lax.axis_index("tx"), lax.axis_index("ty"), lax.axis_index("ang")
    tx_prev, tx_next = lax.rem(tx + n_tx - 1, n_tx), lax.rem(tx + 1, n_tx)
    early, late = lax.rem(ty, 2) == 0, lax.rem(ty, 2) == 1
    has_above = ty > 0
    late_sends = late & (ty < n_ty - 1)

    barrier = pltpu.get_barrier_semaphore()

    def greet(*device):
        pl.semaphore_signal(barrier, inc=1, device_id=device, device_id_type=MESH)

    for d in range(1, n_ang):
        greet(tx, ty, lax.rem(me + d, n_ang))

    @pl.when(has_above)
    def _():
        greet(tx_next, ty, me)

    @pl.when(early)
    def _():
        greet(tx, ty + 1, me)

    @pl.when(early & has_above)
    def _():
        for a in range(n_ang):
            greet(tx, ty - 1, a)

    small = [
        pltpu.make_async_copy(src, dst, small_sem.at[n])
        for n, (src, dst) in enumerate((
            (angles_hbm, angles_ref), (tilt_hbm, tilt_ref), (offset_hbm, offset_ref),
            (extent_hbm, extent_ref), (feather_hbm, feather_ref),
        ))
    ]
    for copy in small:
        copy.start()
    load_x = pltpu.make_async_copy(x_hbm, x_buf, load_sem.at[0])
    load_g = pltpu.make_async_copy(g_hbm, g_buf, load_sem.at[1])
    load_t = pltpu.make_async_copy(t_hbm, t_buf, load_sem.at[2])
    load_x.start()
    load_g.start()
    load_t.start()

    small[0].wait()
    small[1].wait()
    lean = tilt_ref[0, 0]
    rows_i = lax.broadcasted_iota(jnp.int32, (views, views), 0)
    cols_i = lax.broadcasted_iota(jnp.int32, (views, views), 1)
    spread = jnp.where(rows_i == cols_i, jnp.broadcast_to(angles_ref[...], (views, views)), 0.0)
    theta = jnp.broadcast_to(jnp.sum(spread, axis=1, keepdims=True), (views, BLOCK))
    cth, sth = cos_sin_angle(theta)
    col_buf[...] = sth * lean
    zcoef = cth * (lean * (0.5 * PITCH / U))
    band = 4
    sub = lax.broadcasted_iota(jnp.int32, (8, BLOCK), 0)
    ycoord = jnp.where(sub < band, sub, sub + (U - 2 * band)) - U // 2
    ycoef = ycoord.astype(jnp.float32) * (1.0 / U)
    lane = lax.broadcasted_iota(jnp.int32, (8, BLOCK), 1)
    for i in range(4):
        at = slice(BLOCK * i, BLOCK * (i + 1))
        freq8 = (lane * 2 + (2 * BLOCK * (i % 2) + i // 2)).astype(jnp.float32)
        freq = jnp.concatenate([freq8] * (views // 8), axis=0)
        c1, s1 = cos_sin_turns(zcoef * freq)
        c2, s2 = 1.0 - 2.0 * (s1 * s1), 2.0 * (s1 * c1)
        c, s = c1, s1
        for j in range(4):
            zcos[j, :, at] = c
            zsin[j, :, at] = s
            if j < 3:
                c, s = c * c2 - s * s2, c * s2 + s * c2
        for k in range(views):
            slope = jnp.broadcast_to(col_buf[k : k + 1, :], (8, BLOCK)) * ycoef
            c, s = cos_sin_turns(slope * freq8)
            ycos[8 * k : 8 * k + 8, at] = c
            ysin[8 * k : 8 * k + 8, at] = s

    load_x.wait()
    load_g.wait()
    rows = views * 8
    left = x_buf[:, :, : U // 2].reshape(rows, U // 2)
    right = x_buf[:, :, U // 2 :].reshape(rows, U // 2)
    spec_buf[...] = jnp.dot(
        jnp.concatenate([left, right], axis=0), g_buf[...], preferred_element_type=jnp.float32
    )

    for i in range(4):
        at = slice(BLOCK * i, BLOCK * (i + 1))
        at_im = slice(F + BLOCK * i, F + BLOCK * (i + 1))
        acc = [[jnp.zeros((8, BLOCK), jnp.float32) for _ in range(4)] for _ in range(4)]
        for k in range(views):
            here, there = slice(8 * k, 8 * k + 8), slice(rows + 8 * k, rows + 8 * k + 8)
            if i < 2:
                s_re = spec_buf[here, at] + spec_buf[there, at]
                s_im = spec_buf[here, at_im] + spec_buf[there, at_im]
            else:
                s_re = spec_buf[here, at] - spec_buf[there, at]
                s_im = spec_buf[here, at_im] - spec_buf[there, at_im]
            yc, ys = ycos[here, at], ysin[here, at]
            p_re = s_re * yc - s_im * ys
            p_im = s_re * ys + s_im * yc
            for j in range(4):
                c = jnp.broadcast_to(zcos[j, k : k + 1, at], (8, BLOCK))
                s = jnp.broadcast_to(zsin[j, k : k + 1, at], (8, BLOCK))
                acc[j][0] += c * p_re
                acc[j][1] += c * p_im
                acc[j][2] += s * p_re
                acc[j][3] += s * p_im
        part, col = i // 2, BLOCK * (i % 2)
        for j in range(4):
            c_re, c_im, s_re, s_im = acc[j]
            for plane, re, im in (
                (4 + j, c_re - s_im, c_im + s_re),
                (3 - j, c_re + s_im, c_im - s_re),
            ):
                at_row = slice(8 * plane, 8 * plane + 8)
                q_buf[part, at_row, col : col + BLOCK] = re
                q_buf[part, at_row, F // 2 + col : F // 2 + col + BLOCK] = im

    load_t.wait()
    halves = []
    for part in range(2):
        q = q_buf[part]
        high = q.astype(jnp.bfloat16)
        low = (q - high.astype(jnp.float32)).astype(jnp.bfloat16)
        both = jnp.dot(
            jnp.concatenate([high, low], axis=0), t_buf[part], preferred_element_type=jnp.float32
        )
        halves.append(both[: 8 * 8] + both[8 * 8 :])
    first, second = halves[0] + halves[1], halves[0] - halves[1]
    sub_wide = lax.broadcasted_iota(jnp.int32, (8, F), 0)
    upper = sub_wide < band
    for plane in range(8):
        a, b = first[8 * plane : 8 * plane + 8], second[8 * plane : 8 * plane + 8]
        bot[plane] = jnp.where(upper, pltpu.roll(a, band, 0), b)
        top[plane] = jnp.where(upper, a, pltpu.roll(b, band, 0))

    greeted = n_ang - 1 + has_above.astype(jnp.int32) + late.astype(jnp.int32)
    pl.semaphore_wait(barrier, greeted + n_ang * late_sends.astype(jnp.int32))

    bands = ((0, bot, bot_in), (1, top, top_in))

    def piece(which, src, dst, plane, origin):
        return pltpu.make_async_remote_copy(
            src_ref=src.at[plane], dst_ref=dst.at[origin],
            send_sem=send_sem.at[which, plane], recv_sem=recv_sem.at[which, origin],
            device_id=(tx, ty, plane), device_id_type=MESH,
        )

    def exchange(order):
        for plane, band_of in order:
            @pl.when(plane != me)
            def _(plane=plane, band_of=band_of):
                piece(*band_of, plane, me).start()

    def gathered(which, src, dst):
        total = src[me]
        for d in range(1, n_ang):
            origin = lax.rem(me + d, n_ang)
            piece(which, src, dst, me, origin).wait_recv()
            total += dst[origin]
        return total

    def straight(plane, origin):
        return pltpu.make_async_remote_copy(
            src_ref=bot.at[plane], dst_ref=cross_in.at[origin],
            send_sem=send_sem.at[2, plane], recv_sem=recv_sem.at[2, origin],
            device_id=(tx, ty + 1, plane), device_id_type=MESH,
        )

    down = pltpu.make_async_remote_copy(
        src_ref=bot_sum, dst_ref=below_buf, send_sem=send_sem.at[3, 0], recv_sem=recv_sem.at[3, 0],
        device_id=(tx, ty + 1, me), device_id_type=MESH,
    )
    across = pltpu.make_async_remote_copy(
        src_ref=below_buf.at[:, pl.ds(0, BLOCK)], dst_ref=corner_in,
        send_sem=send_sem.at[3, 1], recv_sem=recv_sem.at[3, 1],
        device_id=(tx_prev, ty, me), device_id_type=MESH,
    )

    @pl.when(late)
    def _():
        pl.semaphore_signal(ready_sem, inc=1, device_id=(tx, ty - 1, me), device_id_type=MESH)

    @pl.when(late_sends)
    def _():
        for plane in range(n_ang):
            straight(plane, me).start()

    @pl.when(early)
    def _():
        exchange([(p, b) for p in range(3) for b in bands] + [(p, b) for b in bands for p in range(3, n_ang)])

    @pl.when(late)
    def _():
        exchange([(p, b) for b in bands for p in range(n_ang)])

    bottom = gathered(*bands[0])
    bot_sum[...] = bottom
    @pl.when(early)
    def _():
        pl.semaphore_wait(ready_sem, 1)
        down.start()

    lower_ref[:, :F] = bottom[:band]
    lower_ref[:, F:] = pltpu.roll(bottom, band, 0)[:band]
    top_sum[...] = gathered(*bands[1])

    @pl.when(late)
    def _():
        down.wait_recv()

    @pl.when(early & has_above)
    def _():
        total = None
        for origin in range(n_ang):
            straight(me, origin).wait_recv()
            total = cross_in[origin] if total is None else total + cross_in[origin]
        below_buf[...] = total

    @pl.when(ty == 0)
    def _():
        below_buf[...] = jnp.zeros_like(below_buf)

    @pl.when(has_above)
    def _():
        across.start()

    for copy in small[2:]:
        copy.wait()
    row = sub % band
    own = jnp.zeros((8, BLOCK), jnp.float32)
    other = jnp.zeros((8, BLOCK), jnp.float32)
    seen = (ty > 0).astype(jnp.int32)
    for r in range(band):
        a = feather_ref[0, 0, r].astype(jnp.float32)
        b = (feather_ref[0, 1, r] * (r < extent_ref[0, 0]).astype(jnp.int32) * seen).astype(jnp.float32)
        own = jnp.where(row == r, a, own)
        other = jnp.where(row == r, b, other)
    total = jnp.maximum(own + other, 1.0)
    own, other = own / total, other / total
    shift = offset_ref[0, 0]
    turn_by = (BLOCK - shift) & (BLOCK - 1)

    @pl.when(has_above)
    def _():
        across.wait_recv()

    own_top = top_sum[...]
    below = below_buf[...]
    corner = jnp.where((tx < n_tx - 1) & has_above, corner_in[...], 0.0)
    tail = pltpu.roll(jnp.where(sub < band, corner, below[:, :BLOCK]), band, 0)
    pieces = [below[:, BLOCK * i : BLOCK * (i + 1)] for i in range(4)] + [tail]
    turned = [pltpu.roll(piece, turn_by, 1) for piece in pieces]
    for i in range(4):
        aligned = jnp.where(lane < BLOCK - shift, turned[i], turned[i + 1])
        seam = own * own_top[:, BLOCK * i : BLOCK * (i + 1)] + other * aligned
        seams_ref[:, BLOCK * i : BLOCK * (i + 1)] = seam[:band]
        seams_ref[:, F + BLOCK * i : F + BLOCK * (i + 1)] = pltpu.roll(seam, band, 0)[:band]

    for band_of in bands:
        for d in range(1, n_ang):
            piece(*band_of, lax.rem(me + d, n_ang), me).wait_send()

    @pl.when(late_sends)
    def _():
        for plane in range(n_ang):
            straight(plane, me).wait_send()

    @pl.when(early)
    def _():
        down.wait_send()

    @pl.when(has_above)
    def _():
        across.wait_send()


def hand_over(seams_in, lower_in, seams_ref, lower_ref, sem):
    copies = [
        pltpu.make_async_copy(seams_in, seams_ref, sem.at[0]),
        pltpu.make_async_copy(lower_in, lower_ref, sem.at[1]),
    ]
    for copy in copies:
        copy.start()
    for copy in copies:
        copy.wait()


def solution(mesh):
    sizes = tuple(mesh.shape[name] for name in ("tx", "ty", "ang"))
    n_ang = sizes[2]

    def on_device(projections, view_angles, tilt, offsets, extents, feather):
        _, _, views, rows, width = projections.shape
        band = rows // 2
        g = jnp.asarray(forward_half_table())
        t = jnp.asarray(inverse_half_tables(views * n_ang))
        vmem = pl.BlockSpec(memory_space=pltpu.VMEM)
        hbm = pl.BlockSpec(memory_space=pltpu.HBM)
        f32 = jnp.float32
        results = pl.pallas_call(
            functools.partial(kernel, sizes, views),
            out_shape=[pltpu.VMEM((band, width), f32)] * 2,
            in_specs=[hbm] * 8,
            out_specs=[vmem, vmem],
            scratch_shapes=[
                pltpu.VMEM((1, views), f32),
                pltpu.SMEM((1, 1), f32),
                pltpu.SMEM((1, 1), jnp.int32),
                pltpu.SMEM((1, 1), jnp.int32),
                pltpu.SMEM((1, 2, band), jnp.int32),
                pltpu.VMEM((views, rows, width), jnp.bfloat16),
                pltpu.VMEM((F, width), jnp.bfloat16),
                pltpu.VMEM((2, F, F), jnp.bfloat16),
                pltpu.VMEM((2 * views * rows, width), f32),
                pltpu.VMEM((views * rows, F), f32),
                pltpu.VMEM((views * rows, F), f32),
                pltpu.VMEM((4, views, F), f32),
                pltpu.VMEM((4, views, F), f32),
                pltpu.VMEM((views, BLOCK), f32),
                pltpu.VMEM((2, n_ang * rows, F), f32),
                pltpu.VMEM((n_ang, rows, F), f32),
                pltpu.VMEM((n_ang, rows, F), f32),
                pltpu.VMEM((n_ang, rows, F), f32),
                pltpu.VMEM((n_ang, rows, F), f32),
                pltpu.VMEM((rows, F), f32),
                pltpu.VMEM((rows, F), f32),
                pltpu.VMEM((n_ang, rows, F), f32),
                pltpu.VMEM((rows, F), f32),
                pltpu.VMEM((rows, BLOCK), f32),
                pltpu.SemaphoreType.DMA((3,)),
                pltpu.SemaphoreType.DMA((5,)),
                pltpu.SemaphoreType.DMA((4, n_ang)),
                pltpu.SemaphoreType.DMA((4, n_ang)),
                pltpu.SemaphoreType.REGULAR,
            ],
            compiler_params=pltpu.CompilerParams(collective_id=0, has_side_effects=True),
        )(projections[0, 0], g, t, view_angles[0], tilt, offsets, extents, feather[0])
        anywhere = pl.BlockSpec(memory_space=pl.ANY)
        seams, lower = pl.pallas_call(
            hand_over,
            out_shape=[jax.ShapeDtypeStruct((band, width), f32)] * 2,
            in_specs=[anywhere] * 2,
            out_specs=[anywhere] * 2,
            scratch_shapes=[pltpu.SemaphoreType.DMA((2,))],
        )(*(pltpu.with_memory_space_constraint(r, pltpu.VMEM) for r in results))
        return (seams[None, None, None], lower[None, None, None])

    in_specs = (
        P("tx", "ty", "ang", None, None),
        P("tx", "ty", "ang"),
        P("tx", "ty"),
        P("tx", "ty"),
        P("tx", "ty"),
        P("tx", "ty", None, None),
    )
    out_specs = (P("tx", "ty", "ang", None, None), P("tx", "ty", "ang", None, None))
    return jax.shard_map(
        on_device, mesh=mesh, in_specs=in_specs, out_specs=out_specs, check_vma=False
    )
```

```python
import functools
import math

import jax
import jax.numpy as jnp
import ml_dtypes
import numpy as np
from jax import lax
from jax.experimental import pallas as pl
from jax.experimental.pallas import tpu as pltpu
from jax.sharding import PartitionSpec as P

MESH = pl.DeviceIdType.MESH
PITCH = 16.0
U = 1024
F = U // 2
BLOCK = 128
DXMAX = 128

SIN_HALF = (3.1415926401307073, -5.167710083507923, 2.5500775232148563, -0.5982912856211671, 0.07765766030589402)
COS_HALF = (0.9999999532476085, -4.934792830619664, 4.058411352862771, -1.3318765680813944, 0.21968961109803095)


def frequency_order():
    return np.concatenate([np.arange(0, F, 2), np.arange(1, F, 2)])


def forward_half_table():
    freq = frequency_order()[None, :]
    column = np.arange(U // 2)[:, None]
    turn = (column * freq % U) * (2.0 * math.pi / U)
    filt = (freq + 0.5) / F / math.sqrt(U)
    both = np.concatenate([np.cos(turn) * filt, -np.sin(turn) * filt], axis=1)
    return both.astype(np.float32).astype(ml_dtypes.bfloat16)


def inverse_half_tables(views):
    scale = math.sqrt(2.0 / U) / math.sqrt(views)
    place = np.arange(U // 2)[None, :]
    halves = []
    for start in (0, 1):
        freq = np.arange(start, F, 2)[:, None]
        turn = (freq * place % U) * (2.0 * math.pi / U)
        halves.append(np.concatenate([np.cos(turn), -np.sin(turn)], axis=0) * scale)
    return np.stack(halves).astype(np.float32).astype(ml_dtypes.bfloat16)


def horner(z, coefficients):
    total = jnp.full_like(z, coefficients[-1])
    for c in coefficients[-2::-1]:
        total = total * z + c
    return total


def cos_sin_turns(t):
    r = t - jnp.round(t)
    z = r * r
    s = r * horner(z, SIN_HALF)
    c = horner(z, COS_HALF)
    return 1.0 - 2.0 * (s * s), 2.0 * (s * c)


def cos_sin_angle(theta):
    h = theta * 0.5
    z = h * h
    s = h * horner(z, [(-1.0) ** n / math.factorial(2 * n + 1) for n in range(8)])
    c = horner(z, [(-1.0) ** n / math.factorial(2 * n) for n in range(9)])
    return 1.0 - 2.0 * (s * s), 2.0 * (s * c)


def kernel(
    sizes, views,
    x_hbm, g_hbm, t_hbm, angles_hbm, tilt_hbm, offset_hbm, extent_hbm, feather_hbm,
    seams_ref, lower_ref,
    angles_ref, tilt_ref, offset_ref, extent_ref, feather_ref, x_buf, g_buf, t_buf, spec_buf, ycos, ysin, zcos, zsin, col_buf, q_buf,
    bot, top, bot_near, top_near, bot_pair, top_pair, bot_mid, top_mid, bot_four, top_four, bot_last, top_last, bot_far, top_far,
    bot_sum, top_sum, cross_in, corners_in, below_buf, corner_sum,
    load_sem, small_sem, send_sem, recv_sem, ready_sem,
):
    n_tx, n_ty, n_ang = sizes
    tx, ty, me = lax.axis_index("tx"), lax.axis_index("ty"), lax.axis_index("ang")
    tx_prev, tx_next = lax.rem(tx + n_tx - 1, n_tx), lax.rem(tx + 1, n_tx)
    early, late = lax.rem(ty, 2) == 0, lax.rem(ty, 2) == 1
    has_above = ty > 0
    late_sends = late & (ty < n_ty - 1)

    barrier = pltpu.get_barrier_semaphore()

    def greet(*device):
        pl.semaphore_signal(barrier, inc=1, device_id=device, device_id_type=MESH)

    bits = [lax.rem(me, 2), lax.rem(me // 2, 2), me // 4]
    partners = [me + step * (1 - 2 * bit) for step, bit in zip((1, 2, 4), bits)]
    half, parity = me // 2, bits[0]
    n_pair = n_ang // 2
    greet(tx, ty, partners[0])
    greet(tx, ty, partners[1])
    greet(tx, ty, partners[2])

    @pl.when(late)
    def _():
        greet(tx_next, ty, me)

    @pl.when(early)
    def _():
        greet(tx, ty, partners[1] + partners[2] - me)
        greet(tx, ty + 1, me)

    @pl.when(early & has_above)
    def _():
        for i in range(n_pair):
            greet(tx, ty - 1, 2 * i + parity)
            greet(tx_next, ty - 1, 2 * i + parity)

    small = [
        pltpu.make_async_copy(src, dst, small_sem.at[n])
        for n, (src, dst) in enumerate((
            (angles_hbm, angles_ref), (tilt_hbm, tilt_ref), (offset_hbm, offset_ref),
            (extent_hbm, extent_ref), (feather_hbm, feather_ref),
        ))
    ]
    for copy in small:
        copy.start()
    load_x = pltpu.make_async_copy(x_hbm, x_buf, load_sem.at[0])
    load_g = pltpu.make_async_copy(g_hbm, g_buf, load_sem.at[1])
    load_t = pltpu.make_async_copy(t_hbm, t_buf, load_sem.at[2])
    load_x.start()
    load_g.start()
    load_t.start()

    small[0].wait()
    small[1].wait()
    lean = tilt_ref[0, 0]
    rows_i = lax.broadcasted_iota(jnp.int32, (views, views), 0)
    cols_i = lax.broadcasted_iota(jnp.int32, (views, views), 1)
    spread = jnp.where(rows_i == cols_i, jnp.broadcast_to(angles_ref[...], (views, views)), 0.0)
    theta = jnp.broadcast_to(jnp.sum(spread, axis=1, keepdims=True), (views, BLOCK))
    cth, sth = cos_sin_angle(theta)
    col_buf[...] = sth * lean
    zcoef = cth * (lean * (0.5 * PITCH / U))
    band = 4
    sub = lax.broadcasted_iota(jnp.int32, (8, BLOCK), 0)
    ycoord = jnp.where(sub < band, sub, sub + (U - 2 * band)) - U // 2
    ycoef = ycoord.astype(jnp.float32) * (1.0 / U)
    lane = lax.broadcasted_iota(jnp.int32, (8, BLOCK), 1)
    for i in range(4):
        at = slice(BLOCK * i, BLOCK * (i + 1))
        freq8 = (lane * 2 + (2 * BLOCK * (i % 2) + i // 2)).astype(jnp.float32)
        freq = jnp.concatenate([freq8] * (views // 8), axis=0)
        c1, s1 = cos_sin_turns(zcoef * freq)
        c2, s2 = 1.0 - 2.0 * (s1 * s1), 2.0 * (s1 * c1)
        c, s = c1, s1
        for j in range(4):
            zcos[j, :, at] = c
            zsin[j, :, at] = s
            if j < 3:
                c, s = c * c2 - s * s2, c * s2 + s * c2
        for k in range(views):
            slope = jnp.broadcast_to(col_buf[k : k + 1, :], (8, BLOCK)) * ycoef
            c, s = cos_sin_turns(slope * freq8)
            ycos[8 * k : 8 * k + 8, at] = c
            ysin[8 * k : 8 * k + 8, at] = s

    load_x.wait()
    load_g.wait()
    rows = views * 8
    left = x_buf[:, :, : U // 2].reshape(rows, U // 2)
    right = x_buf[:, :, U // 2 :].reshape(rows, U // 2)
    spec_buf[...] = jnp.dot(
        jnp.concatenate([left, right], axis=0), g_buf[...], preferred_element_type=jnp.float32
    )

    for i in range(4):
        at = slice(BLOCK * i, BLOCK * (i + 1))
        at_im = slice(F + BLOCK * i, F + BLOCK * (i + 1))
        acc = [[jnp.zeros((8, BLOCK), jnp.float32) for _ in range(4)] for _ in range(4)]
        for k in range(views):
            here, there = slice(8 * k, 8 * k + 8), slice(rows + 8 * k, rows + 8 * k + 8)
            if i < 2:
                s_re = spec_buf[here, at] + spec_buf[there, at]
                s_im = spec_buf[here, at_im] + spec_buf[there, at_im]
            else:
                s_re = spec_buf[here, at] - spec_buf[there, at]
                s_im = spec_buf[here, at_im] - spec_buf[there, at_im]
            yc, ys = ycos[here, at], ysin[here, at]
            p_re = s_re * yc - s_im * ys
            p_im = s_re * ys + s_im * yc
            for j in range(4):
                c = jnp.broadcast_to(zcos[j, k : k + 1, at], (8, BLOCK))
                s = jnp.broadcast_to(zsin[j, k : k + 1, at], (8, BLOCK))
                acc[j][0] += c * p_re
                acc[j][1] += c * p_im
                acc[j][2] += s * p_re
                acc[j][3] += s * p_im
        part, col = i // 2, BLOCK * (i % 2)
        for j in range(4):
            c_re, c_im, s_re, s_im = acc[j]
            for plane, re, im in (
                (4 + j, c_re - s_im, c_im + s_re),
                (3 - j, c_re + s_im, c_im - s_re),
            ):
                at_row = slice(8 * plane, 8 * plane + 8)
                q_buf[part, at_row, col : col + BLOCK] = re
                q_buf[part, at_row, F // 2 + col : F // 2 + col + BLOCK] = im

    load_t.wait()
    halves = []
    for part in range(2):
        q = q_buf[part]
        high = q.astype(jnp.bfloat16)
        low = (q - high.astype(jnp.float32)).astype(jnp.bfloat16)
        both = jnp.dot(
            jnp.concatenate([high, low], axis=0), t_buf[part], preferred_element_type=jnp.float32
        )
        halves.append(both[: 8 * 8] + both[8 * 8 :])
    first, second = halves[0] + halves[1], halves[0] - halves[1]
    sub_wide = lax.broadcasted_iota(jnp.int32, (8, F), 0)
    upper = sub_wide < band
    for plane in range(8):
        a, b = first[8 * plane : 8 * plane + 8], second[8 * plane : 8 * plane + 8]
        bot[plane] = jnp.where(upper, pltpu.roll(a, band, 0), b)
        top[plane] = jnp.where(upper, a, pltpu.roll(b, band, 0))

    greeted = n_pair + late.astype(jnp.int32)
    pl.semaphore_wait(barrier, greeted + 2 * n_pair * late_sends.astype(jnp.int32))

    bands = (
        (0, bot, bot_near, bot_pair, bot_mid, bot_four, bot_last),
        (1, top, top_near, top_pair, top_mid, top_four, top_last),
    )
    far_slots = (bot_far, top_far)

    def swap(src, dst, sem, partner):
        return pltpu.make_async_remote_copy(
            src_ref=src, dst_ref=dst, send_sem=send_sem.at[sem], recv_sem=recv_sem.at[sem],
            device_id=(tx, ty, partner), device_id_type=MESH,
        )

    def near(band_of, i):
        which, mine, landed = band_of[:3]
        return swap(mine.at[2 * i + 1 - parity], landed.at[i], 7 * which + i, partners[0])

    def mid(band_of, j):
        which, pair, landed = band_of[0], band_of[3], band_of[4]
        return swap(pair.at[2 * j + 1 - bits[1]], landed.at[j], 7 * which + 4 + j, partners[1])

    def last(band_of):
        which, four, landed = band_of[0], band_of[5], band_of[6]
        return swap(four.at[1 - bits[2]], landed, 7 * which + 6, partners[2])

    def paired(band_of, i):
        _, mine, landed, pair = band_of[:4]
        near(band_of, i).wait_recv()
        pair[i] = mine[2 * i + parity] + landed[i]

    def send_mid(band_of):
        for j in range(n_pair // 2):
            mid(band_of, j).start()

    def send_last(band_of):
        _, _, _, pair, landed, four, _ = band_of
        for j in range(n_pair // 2):
            mid(band_of, j).wait_recv()
            four[j] = pair[2 * j + bits[1]] + landed[j]
        last(band_of).start()

    def gathered(band_of):
        four, landed = band_of[5:]
        last(band_of).wait_recv()
        return four[bits[2]] + landed[...]

    def far(band_of, i, origin):
        which, pair = band_of[0], band_of[3]
        return pltpu.make_async_remote_copy(
            src_ref=pair.at[i], dst_ref=far_slots[which].at[origin],
            send_sem=send_sem.at[24 + 4 * which + i], recv_sem=recv_sem.at[24 + 4 * which + origin],
            device_id=(tx, ty, 2 * i + parity), device_id_type=MESH,
        )

    def send_far(band_of, i):
        @pl.when(i != half)
        def _():
            far(band_of, i, half).start()

    def gathered_far(band_of):
        total = band_of[3][half]
        for d in range(1, n_pair):
            origin = lax.rem(half + d, n_pair)
            far(band_of, half, origin).wait_recv()
            total += far_slots[band_of[0]][origin]
        return total

    def straight(i, origin):
        return pltpu.make_async_remote_copy(
            src_ref=bot_pair.at[i], dst_ref=cross_in.at[origin],
            send_sem=send_sem.at[14 + i], recv_sem=recv_sem.at[14 + origin],
            device_id=(tx, ty + 1, 2 * i + parity), device_id_type=MESH,
        )

    def slanted(i, origin):
        return pltpu.make_async_remote_copy(
            src_ref=bot_pair.at[i, :, pl.ds(0, BLOCK)], dst_ref=corners_in.at[origin],
            send_sem=send_sem.at[18 + i], recv_sem=recv_sem.at[18 + origin],
            device_id=(tx_prev, ty + 1, 2 * i + parity), device_id_type=MESH,
        )

    down = pltpu.make_async_remote_copy(
        src_ref=bot_sum, dst_ref=below_buf, send_sem=send_sem.at[22], recv_sem=recv_sem.at[22],
        device_id=(tx, ty + 1, me), device_id_type=MESH,
    )
    across = pltpu.make_async_remote_copy(
        src_ref=below_buf.at[:, pl.ds(0, BLOCK)], dst_ref=corners_in.at[0],
        send_sem=send_sem.at[23], recv_sem=recv_sem.at[23],
        device_id=(tx_prev, ty, me), device_id_type=MESH,
    )

    @pl.when(late)
    def _():
        pl.semaphore_signal(ready_sem, inc=1, device_id=(tx, ty - 1, me), device_id_type=MESH)

    lower_part, upper_part = bands
    for band_of in bands:
        for i in range(n_pair):
            near(band_of, i).start()

    @pl.when(late)
    def _():
        for i in range(n_pair):
            paired(lower_part, i)

            @pl.when(late_sends)
            def _():
                slanted(i, half).start()
                straight(i, half).start()

        send_mid(lower_part)
        for i in range(n_pair):
            paired(upper_part, i)
        send_mid(upper_part)
        send_last(lower_part)
        send_last(upper_part)
        bot_sum[...] = gathered(lower_part)
        top_sum[...] = gathered(upper_part)

    @pl.when(early)
    def _():
        for band_of in bands:
            for i in range(n_pair):
                paired(band_of, i)
                send_far(band_of, i)
        bot_sum[...] = gathered_far(lower_part)
        pl.semaphore_wait(ready_sem, 1)
        down.start()
        top_sum[...] = gathered_far(upper_part)

    bottom = bot_sum[...]
    lower_ref[:, :F] = bottom[:band]
    lower_ref[:, F:] = pltpu.roll(bottom, band, 0)[:band]

    @pl.when(late)
    def _():
        down.wait_recv()

    @pl.when(early & has_above)
    def _():
        for origin in range(n_pair):
            slanted(half, origin).wait_recv()
            straight(half, origin).wait_recv()
        below_buf[...] = (cross_in[0] + cross_in[1]) + (cross_in[2] + cross_in[3])
        corner_sum[...] = (corners_in[0] + corners_in[1]) + (corners_in[2] + corners_in[3])

    @pl.when(ty == 0)
    def _():
        below_buf[...] = jnp.zeros_like(below_buf)
        corner_sum[...] = jnp.zeros_like(corner_sum)

    @pl.when(late)
    def _():
        across.start()

    for copy in small[2:]:
        copy.wait()
    row = sub % band
    own = jnp.zeros((8, BLOCK), jnp.float32)
    other = jnp.zeros((8, BLOCK), jnp.float32)
    seen = (ty > 0).astype(jnp.int32)
    for r in range(band):
        a = feather_ref[0, 0, r].astype(jnp.float32)
        b = (feather_ref[0, 1, r] * (r < extent_ref[0, 0]).astype(jnp.int32) * seen).astype(jnp.float32)
        own = jnp.where(row == r, a, own)
        other = jnp.where(row == r, b, other)
    total = jnp.maximum(own + other, 1.0)
    own, other = own / total, other / total
    shift = offset_ref[0, 0]
    turn_by = (BLOCK - shift) & (BLOCK - 1)

    @pl.when(late)
    def _():
        across.wait_recv()
        corner_sum[...] = corners_in[0]

    own_top = top_sum[...]
    below = below_buf[...]
    corner = jnp.where(tx < n_tx - 1, corner_sum[...], 0.0)
    tail = pltpu.roll(jnp.where(sub < band, corner, below[:, :BLOCK]), band, 0)
    pieces = [below[:, BLOCK * i : BLOCK * (i + 1)] for i in range(4)] + [tail]
    turned = [pltpu.roll(piece, turn_by, 1) for piece in pieces]
    for i in range(4):
        aligned = jnp.where(lane < BLOCK - shift, turned[i], turned[i + 1])
        seam = own * own_top[:, BLOCK * i : BLOCK * (i + 1)] + other * aligned
        seams_ref[:, BLOCK * i : BLOCK * (i + 1)] = seam[:band]
        seams_ref[:, F + BLOCK * i : F + BLOCK * (i + 1)] = pltpu.roll(seam, band, 0)[:band]

    for band_of in bands:
        for i in range(n_pair):
            near(band_of, i).wait_send()

        @pl.when(late)
        def _():
            for j in range(n_pair // 2):
                mid(band_of, j).wait_send()
            last(band_of).wait_send()

        @pl.when(early)
        def _():
            for d in range(1, n_pair):
                far(band_of, lax.rem(half + d, n_pair), half).wait_send()

    @pl.when(late_sends)
    def _():
        for i in range(n_pair):
            slanted(i, half).wait_send()
            straight(i, half).wait_send()

    @pl.when(early)
    def _():
        down.wait_send()

    @pl.when(late)
    def _():
        across.wait_send()


def hand_over(seams_in, lower_in, seams_ref, lower_ref, sem):
    copies = [
        pltpu.make_async_copy(seams_in, seams_ref, sem.at[0]),
        pltpu.make_async_copy(lower_in, lower_ref, sem.at[1]),
    ]
    for copy in copies:
        copy.start()
    for copy in copies:
        copy.wait()


def solution(mesh):
    sizes = tuple(mesh.shape[name] for name in ("tx", "ty", "ang"))
    n_ang = sizes[2]

    def on_device(projections, view_angles, tilt, offsets, extents, feather):
        _, _, views, rows, width = projections.shape
        band = rows // 2
        g = jnp.asarray(forward_half_table())
        t = jnp.asarray(inverse_half_tables(views * n_ang))
        vmem = pl.BlockSpec(memory_space=pltpu.VMEM)
        hbm = pl.BlockSpec(memory_space=pltpu.HBM)
        f32 = jnp.float32
        results = pl.pallas_call(
            functools.partial(kernel, sizes, views),
            out_shape=[pltpu.VMEM((band, width), f32)] * 2,
            in_specs=[hbm] * 8,
            out_specs=[vmem, vmem],
            scratch_shapes=[
                pltpu.VMEM((1, views), f32),
                pltpu.SMEM((1, 1), f32),
                pltpu.SMEM((1, 1), jnp.int32),
                pltpu.SMEM((1, 1), jnp.int32),
                pltpu.SMEM((1, 2, band), jnp.int32),
                pltpu.VMEM((views, rows, width), jnp.bfloat16),
                pltpu.VMEM((F, width), jnp.bfloat16),
                pltpu.VMEM((2, F, F), jnp.bfloat16),
                pltpu.VMEM((2 * views * rows, width), f32),
                pltpu.VMEM((views * rows, F), f32),
                pltpu.VMEM((views * rows, F), f32),
                pltpu.VMEM((4, views, F), f32),
                pltpu.VMEM((4, views, F), f32),
                pltpu.VMEM((views, BLOCK), f32),
                pltpu.VMEM((2, n_ang * rows, F), f32),
                pltpu.VMEM((n_ang, rows, F), f32),
                pltpu.VMEM((n_ang, rows, F), f32),
                *[pltpu.VMEM((n_ang // 2, rows, F), f32)] * 4,
                *[pltpu.VMEM((n_ang // 4, rows, F), f32)] * 4,
                *[pltpu.VMEM((rows, F), f32)] * 2,
                *[pltpu.VMEM((n_ang // 2, rows, F), f32)] * 2,
                *[pltpu.VMEM((rows, F), f32)] * 2,
                pltpu.VMEM((n_ang // 2, rows, F), f32),
                pltpu.VMEM((n_ang // 2, rows, BLOCK), f32),
                pltpu.VMEM((rows, F), f32),
                pltpu.VMEM((rows, BLOCK), f32),
                pltpu.SemaphoreType.DMA((3,)),
                pltpu.SemaphoreType.DMA((5,)),
                pltpu.SemaphoreType.DMA((32,)),
                pltpu.SemaphoreType.DMA((32,)),
                pltpu.SemaphoreType.REGULAR,
            ],
            compiler_params=pltpu.CompilerParams(collective_id=0, has_side_effects=True),
        )(projections[0, 0], g, t, view_angles[0], tilt, offsets, extents, feather[0])
        anywhere = pl.BlockSpec(memory_space=pl.ANY)
        seams, lower = pl.pallas_call(
            hand_over,
            out_shape=[jax.ShapeDtypeStruct((band, width), f32)] * 2,
            in_specs=[anywhere] * 2,
            out_specs=[anywhere] * 2,
            scratch_shapes=[pltpu.SemaphoreType.DMA((2,))],
        )(*(pltpu.with_memory_space_constraint(r, pltpu.VMEM) for r in results))
        return (seams[None, None, None], lower[None, None, None])

    in_specs = (
        P("tx", "ty", "ang", None, None),
        P("tx", "ty", "ang"),
        P("tx", "ty"),
        P("tx", "ty"),
        P("tx", "ty"),
        P("tx", "ty", None, None),
    )
    out_specs = (P("tx", "ty", "ang", None, None), P("tx", "ty", "ang", None, None))
    return jax.shard_map(
        on_device, mesh=mesh, in_specs=in_specs, out_specs=out_specs, check_vma=False
    )
```

```python
import functools
import math

import jax
import jax.numpy as jnp
import ml_dtypes
import numpy as np
from jax import lax
from jax.experimental import pallas as pl
from jax.experimental.pallas import tpu as pltpu
from jax.sharding import PartitionSpec as P

MESH = pl.DeviceIdType.MESH
PITCH = 16.0
U = 1024
F = U // 2
BLOCK = 128
DXMAX = 128

SIN_HALF = (3.1415926401307073, -5.167710083507923, 2.5500775232148563, -0.5982912856211671, 0.07765766030589402)
COS_HALF = (0.9999999532476085, -4.934792830619664, 4.058411352862771, -1.3318765680813944, 0.21968961109803095)


def frequency_order():
    return np.concatenate([np.arange(0, F, 2), np.arange(1, F, 2)])


def forward_half_table():
    freq = frequency_order()[None, :]
    column = np.arange(U // 2)[:, None]
    turn = (column * freq % U) * (2.0 * math.pi / U)
    filt = (freq + 0.5) / F / math.sqrt(U)
    both = np.concatenate([np.cos(turn) * filt, -np.sin(turn) * filt], axis=1)
    return both.astype(np.float32).astype(ml_dtypes.bfloat16)


def inverse_half_tables(views):
    scale = math.sqrt(2.0 / U) / math.sqrt(views)
    place = np.arange(U // 2)[None, :]
    halves = []
    for start in (0, 1):
        freq = np.arange(start, F, 2)[:, None]
        turn = (freq * place % U) * (2.0 * math.pi / U)
        halves.append(np.concatenate([np.cos(turn), -np.sin(turn)], axis=0) * scale)
    return np.stack(halves).astype(np.float32).astype(ml_dtypes.bfloat16)


def horner(z, coefficients):
    total = jnp.full_like(z, coefficients[-1])
    for c in coefficients[-2::-1]:
        total = total * z + c
    return total


def cos_sin_turns(t):
    r = t - jnp.round(t)
    z = r * r
    s = r * horner(z, SIN_HALF)
    c = horner(z, COS_HALF)
    return 1.0 - 2.0 * (s * s), 2.0 * (s * c)


def cos_sin_angle(theta):
    h = theta * 0.5
    z = h * h
    s = h * horner(z, [(-1.0) ** n / math.factorial(2 * n + 1) for n in range(8)])
    c = horner(z, [(-1.0) ** n / math.factorial(2 * n) for n in range(9)])
    return 1.0 - 2.0 * (s * s), 2.0 * (s * c)


def kernel(
    sizes, views,
    x_hbm, g_hbm, t_hbm, angles_hbm, tilt_hbm, offset_hbm, extent_hbm, feather_hbm,
    seams_ref, lower_ref,
    angles_ref, tilt_ref, offset_ref, extent_ref, feather_ref, x_buf, g_buf, t_buf, spec_buf, ycos, ysin, zcos, zsin, col_buf, q_buf,
    bot, top, bot_near, top_near, bot_pair, top_pair, bot_mid, top_mid, bot_four, top_four, bot_last, top_last, bot_far, top_far,
    bot_sum, top_sum, cross_in, corners_in, below_buf, corner_sum,
    load_sem, small_sem, send_sem, recv_sem, ready_sem,
):
    n_tx, n_ty, n_ang = sizes
    tx, ty, me = lax.axis_index("tx"), lax.axis_index("ty"), lax.axis_index("ang")
    tx_prev, tx_next = lax.rem(tx + n_tx - 1, n_tx), lax.rem(tx + 1, n_tx)
    early, late = lax.rem(ty, 2) == 0, lax.rem(ty, 2) == 1
    has_above = ty > 0
    late_sends = late & (ty < n_ty - 1)

    small = [
        pltpu.make_async_copy(src, dst, small_sem.at[n])
        for n, (src, dst) in enumerate((
            (angles_hbm, angles_ref), (tilt_hbm, tilt_ref), (offset_hbm, offset_ref),
            (extent_hbm, extent_ref), (feather_hbm, feather_ref),
        ))
    ]
    for copy in small:
        copy.start()
    load_x = pltpu.make_async_copy(x_hbm, x_buf, load_sem.at[0])
    load_g = pltpu.make_async_copy(g_hbm, g_buf, load_sem.at[1])
    load_t = pltpu.make_async_copy(t_hbm, t_buf, load_sem.at[2])
    load_x.start()
    load_g.start()
    load_t.start()

    barrier = pltpu.get_barrier_semaphore()

    def greet(*device):
        pl.semaphore_signal(barrier, inc=1, device_id=device, device_id_type=MESH)

    bits = [lax.rem(me, 2), lax.rem(me // 2, 2), me // 4]
    partners = [me + step * (1 - 2 * bit) for step, bit in zip((1, 2, 4), bits)]
    half, parity = me // 2, bits[0]
    n_pair = n_ang // 2
    greet(tx, ty, partners[0])
    greet(tx, ty, partners[1])
    greet(tx, ty, partners[2])

    @pl.when(late)
    def _():
        greet(tx_next, ty, me)

    @pl.when(early)
    def _():
        greet(tx, ty, partners[1] + partners[2] - me)
        greet(tx, ty + 1, me)

    @pl.when(early & has_above)
    def _():
        for i in range(n_pair):
            greet(tx, ty - 1, 2 * i + parity)
            greet(tx_next, ty - 1, 2 * i + parity)

    small[0].wait()
    small[1].wait()
    lean = tilt_ref[0, 0]
    rows_i = lax.broadcasted_iota(jnp.int32, (views, views), 0)
    cols_i = lax.broadcasted_iota(jnp.int32, (views, views), 1)
    spread = jnp.where(rows_i == cols_i, jnp.broadcast_to(angles_ref[...], (views, views)), 0.0)
    theta = jnp.broadcast_to(jnp.sum(spread, axis=1, keepdims=True), (views, BLOCK))
    cth, sth = cos_sin_angle(theta)
    col_buf[...] = sth * lean
    zcoef = cth * (lean * (0.5 * PITCH / U))
    band = 4
    sub = lax.broadcasted_iota(jnp.int32, (8, BLOCK), 0)
    ycoord = jnp.where(sub < band, sub, sub + (U - 2 * band)) - U // 2
    ycoef = ycoord.astype(jnp.float32) * (1.0 / U)
    lane = lax.broadcasted_iota(jnp.int32, (8, BLOCK), 1)
    for i in range(4):
        at = slice(BLOCK * i, BLOCK * (i + 1))
        freq8 = (lane * 2 + (2 * BLOCK * (i % 2) + i // 2)).astype(jnp.float32)
        freq = jnp.concatenate([freq8] * (views // 8), axis=0)
        c1, s1 = cos_sin_turns(zcoef * freq)
        c2, s2 = 1.0 - 2.0 * (s1 * s1), 2.0 * (s1 * c1)
        c, s = c1, s1
        for j in range(4):
            zcos[j, :, at] = c
            zsin[j, :, at] = s
            if j < 3:
                c, s = c * c2 - s * s2, c * s2 + s * c2
        for k in range(views):
            slope = jnp.broadcast_to(col_buf[k : k + 1, :], (8, BLOCK)) * ycoef
            c, s = cos_sin_turns(slope * freq8)
            ycos[8 * k : 8 * k + 8, at] = c
            ysin[8 * k : 8 * k + 8, at] = s

    load_x.wait()
    load_g.wait()
    rows = views * 8
    left = x_buf[:, :, : U // 2].reshape(rows, U // 2)
    right = x_buf[:, :, U // 2 :].reshape(rows, U // 2)
    spec_buf[...] = jnp.dot(
        jnp.concatenate([left, right], axis=0), g_buf[...], preferred_element_type=jnp.float32
    )

    for i in range(4):
        at = slice(BLOCK * i, BLOCK * (i + 1))
        at_im = slice(F + BLOCK * i, F + BLOCK * (i + 1))
        acc = [[jnp.zeros((8, BLOCK), jnp.float32) for _ in range(4)] for _ in range(4)]
        for k in range(views):
            here, there = slice(8 * k, 8 * k + 8), slice(rows + 8 * k, rows + 8 * k + 8)
            if i < 2:
                s_re = spec_buf[here, at] + spec_buf[there, at]
                s_im = spec_buf[here, at_im] + spec_buf[there, at_im]
            else:
                s_re = spec_buf[here, at] - spec_buf[there, at]
                s_im = spec_buf[here, at_im] - spec_buf[there, at_im]
            yc, ys = ycos[here, at], ysin[here, at]
            p_re = s_re * yc - s_im * ys
            p_im = s_re * ys + s_im * yc
            for j in range(4):
                c = jnp.broadcast_to(zcos[j, k : k + 1, at], (8, BLOCK))
                s = jnp.broadcast_to(zsin[j, k : k + 1, at], (8, BLOCK))
                acc[j][0] += c * p_re
                acc[j][1] += c * p_im
                acc[j][2] += s * p_re
                acc[j][3] += s * p_im
        part, col = i // 2, BLOCK * (i % 2)
        for j in range(4):
            c_re, c_im, s_re, s_im = acc[j]
            for plane, re, im in (
                (4 + j, c_re - s_im, c_im + s_re),
                (3 - j, c_re + s_im, c_im - s_re),
            ):
                at_row = slice(8 * plane, 8 * plane + 8)
                q_buf[part, at_row, col : col + BLOCK] = re
                q_buf[part, at_row, F // 2 + col : F // 2 + col + BLOCK] = im

    load_t.wait()
    halves = []
    for part in range(2):
        q = q_buf[part]
        high = q.astype(jnp.bfloat16)
        low = (q - high.astype(jnp.float32)).astype(jnp.bfloat16)
        both = jnp.dot(
            jnp.concatenate([high, low], axis=0), t_buf[part], preferred_element_type=jnp.float32
        )
        halves.append(both[: 8 * 8] + both[8 * 8 :])
    first, second = halves[0] + halves[1], halves[0] - halves[1]
    sub_wide = lax.broadcasted_iota(jnp.int32, (8, F), 0)
    upper = sub_wide < band
    for plane in range(8):
        a, b = first[8 * plane : 8 * plane + 8], second[8 * plane : 8 * plane + 8]
        bot[plane] = jnp.where(upper, pltpu.roll(a, band, 0), b)
        top[plane] = jnp.where(upper, a, pltpu.roll(b, band, 0))

    greeted = n_pair + late.astype(jnp.int32)
    pl.semaphore_wait(barrier, greeted + 2 * n_pair * late_sends.astype(jnp.int32))

    bands = (
        (0, bot, bot_near, bot_pair, bot_mid, bot_four, bot_last),
        (1, top, top_near, top_pair, top_mid, top_four, top_last),
    )
    far_slots = (bot_far, top_far)

    def swap(src, dst, sem, partner):
        return pltpu.make_async_remote_copy(
            src_ref=src, dst_ref=dst, send_sem=send_sem.at[sem], recv_sem=recv_sem.at[sem],
            device_id=(tx, ty, partner), device_id_type=MESH,
        )

    def near(band_of, i):
        which, mine, landed = band_of[:3]
        return swap(mine.at[2 * i + 1 - parity], landed.at[i], 7 * which + i, partners[0])

    def mid(band_of, j):
        which, pair, landed = band_of[0], band_of[3], band_of[4]
        return swap(pair.at[2 * j + 1 - bits[1]], landed.at[j], 7 * which + 4 + j, partners[1])

    def last(band_of):
        which, four, landed = band_of[0], band_of[5], band_of[6]
        return swap(four.at[1 - bits[2]], landed, 7 * which + 6, partners[2])

    def paired(band_of, i):
        _, mine, landed, pair = band_of[:4]
        near(band_of, i).wait_recv()
        pair[i] = mine[2 * i + parity] + landed[i]

    def four(band_of, j):
        _, _, _, pair, landed, fours, _ = band_of
        mid(band_of, j).wait_recv()
        fours[j] = pair[2 * j + bits[1]] + landed[j]

    def send_last(band_of):
        four(band_of, 1 - bits[2])
        last(band_of).start()

    def gathered(band_of):
        fours, landed = band_of[5:]
        four(band_of, bits[2])
        last(band_of).wait_recv()
        return fours[bits[2]] + landed[...]

    def far(band_of, i, origin):
        which, pair = band_of[0], band_of[3]
        return pltpu.make_async_remote_copy(
            src_ref=pair.at[i], dst_ref=far_slots[which].at[origin],
            send_sem=send_sem.at[24 + 4 * which + i], recv_sem=recv_sem.at[24 + 4 * which + origin],
            device_id=(tx, ty, 2 * i + parity), device_id_type=MESH,
        )

    def send_far(band_of, i):
        @pl.when(i != half)
        def _():
            far(band_of, i, half).start()

    def gathered_far(band_of):
        total = band_of[3][half]
        for d in range(1, n_pair):
            origin = lax.rem(half + d, n_pair)
            far(band_of, half, origin).wait_recv()
            total += far_slots[band_of[0]][origin]
        return total

    def straight(i, origin):
        return pltpu.make_async_remote_copy(
            src_ref=bot_pair.at[i], dst_ref=cross_in.at[origin],
            send_sem=send_sem.at[14 + i], recv_sem=recv_sem.at[14 + origin],
            device_id=(tx, ty + 1, 2 * i + parity), device_id_type=MESH,
        )

    def slanted(i, origin):
        return pltpu.make_async_remote_copy(
            src_ref=bot_pair.at[i, pl.ds(0, 4), pl.ds(0, BLOCK)], dst_ref=corners_in.at[origin, pl.ds(0, 4)],
            send_sem=send_sem.at[18 + i], recv_sem=recv_sem.at[18 + origin],
            device_id=(tx_prev, ty + 1, 2 * i + parity), device_id_type=MESH,
        )

    down = pltpu.make_async_remote_copy(
        src_ref=bot_sum, dst_ref=below_buf, send_sem=send_sem.at[22], recv_sem=recv_sem.at[22],
        device_id=(tx, ty + 1, me), device_id_type=MESH,
    )
    across = pltpu.make_async_remote_copy(
        src_ref=below_buf.at[:, pl.ds(0, BLOCK)], dst_ref=corners_in.at[0],
        send_sem=send_sem.at[23], recv_sem=recv_sem.at[23],
        device_id=(tx_prev, ty, me), device_id_type=MESH,
    )

    @pl.when(late)
    def _():
        pl.semaphore_signal(ready_sem, inc=1, device_id=(tx, ty - 1, me), device_id_type=MESH)

    lower_part, upper_part = bands
    held = [late & (parity == 0) & (half < 2), late & (parity == 0) & (half >= 2)]
    plans = ({2: (0, 1, 2, 3)}, {1: (1, 2), 2: (3,)})
    for i in range(n_pair):
        near(lower_part, i).start()

    for i in range(n_pair):
        @pl.when((late & (parity == 1)) | (held[1] & (i < 1)))
        def _():
            near(upper_part, i).start()

    @pl.when(late)
    def _():
        for i in range(n_pair):
            for group, plan in zip(held, plans):
                @pl.when(group)
                def _(plan=plan):
                    for k in plan.get(i, ()):
                        near(upper_part, k).start()

            paired(lower_part, i)

            @pl.when(late_sends)
            def _():
                slanted(i, half).start()
                straight(i, half).start()

        for j in range(n_pair // 2):
            mid(lower_part, j).start()
        for i in range(n_pair):
            paired(upper_part, i)
            if i % 2:
                mid(upper_part, i // 2).start()
        send_last(lower_part)
        send_last(upper_part)
        bot_sum[...] = gathered(lower_part)
        top_sum[...] = gathered(upper_part)

    @pl.when(early)
    def _():
        for i in range(n_pair):
            paired(lower_part, i)
            send_far(lower_part, i)
            if i == 3:
                for n in range(n_pair):
                    near(upper_part, n).start()
        for i in range(n_pair):
            paired(upper_part, i)
            send_far(upper_part, i)
        bot_sum[...] = gathered_far(lower_part)
        pl.semaphore_wait(ready_sem, 1)
        down.start()
        top_sum[...] = gathered_far(upper_part)

    bottom = bot_sum[...]
    lower_ref[:, :F] = bottom[:band]
    lower_ref[:, F:] = pltpu.roll(bottom, band, 0)[:band]

    @pl.when(late)
    def _():
        down.wait_recv()

    @pl.when(early & has_above)
    def _():
        for origin in range(n_pair):
            slanted(half, origin).wait_recv()
            straight(half, origin).wait_recv()
        below_buf[...] = (cross_in[0] + cross_in[1]) + (cross_in[2] + cross_in[3])
        corner_sum[...] = (corners_in[0] + corners_in[1]) + (corners_in[2] + corners_in[3])

    @pl.when(ty == 0)
    def _():
        below_buf[...] = jnp.zeros_like(below_buf)
        corner_sum[...] = jnp.zeros_like(corner_sum)

    @pl.when(late)
    def _():
        across.start()

    for copy in small[2:]:
        copy.wait()
    row = sub % band
    own = jnp.zeros((8, BLOCK), jnp.float32)
    other = jnp.zeros((8, BLOCK), jnp.float32)
    seen = (ty > 0).astype(jnp.int32)
    for r in range(band):
        a = feather_ref[0, 0, r].astype(jnp.float32)
        b = (feather_ref[0, 1, r] * (r < extent_ref[0, 0]).astype(jnp.int32) * seen).astype(jnp.float32)
        own = jnp.where(row == r, a, own)
        other = jnp.where(row == r, b, other)
    total = jnp.maximum(own + other, 1.0)
    own, other = own / total, other / total
    shift = offset_ref[0, 0]
    turn_by = (BLOCK - shift) & (BLOCK - 1)

    @pl.when(late)
    def _():
        across.wait_recv()
        corner_sum[...] = corners_in[0]

    own_top = top_sum[...]
    below = below_buf[...]
    corner = jnp.where(tx < n_tx - 1, corner_sum[...], 0.0)
    tail = pltpu.roll(jnp.where(sub < band, corner, below[:, :BLOCK]), band, 0)
    pieces = [below[:, BLOCK * i : BLOCK * (i + 1)] for i in range(4)] + [tail]
    turned = [pltpu.roll(piece, turn_by, 1) for piece in pieces]
    for i in range(4):
        aligned = jnp.where(lane < BLOCK - shift, turned[i], turned[i + 1])
        seam = own * own_top[:, BLOCK * i : BLOCK * (i + 1)] + other * aligned
        seams_ref[:, BLOCK * i : BLOCK * (i + 1)] = seam[:band]
        seams_ref[:, F + BLOCK * i : F + BLOCK * (i + 1)] = pltpu.roll(seam, band, 0)[:band]

    for band_of in bands:
        for i in range(n_pair):
            near(band_of, i).wait_send()

        @pl.when(late)
        def _():
            for j in range(n_pair // 2):
                mid(band_of, j).wait_send()
            last(band_of).wait_send()

        @pl.when(early)
        def _():
            for d in range(1, n_pair):
                far(band_of, lax.rem(half + d, n_pair), half).wait_send()

    @pl.when(late_sends)
    def _():
        for i in range(n_pair):
            slanted(i, half).wait_send()
            straight(i, half).wait_send()

    @pl.when(early)
    def _():
        down.wait_send()

    @pl.when(late)
    def _():
        across.wait_send()


def hand_over(seams_in, lower_in, seams_ref, lower_ref, sem):
    copies = [
        pltpu.make_async_copy(seams_in, seams_ref, sem.at[0]),
        pltpu.make_async_copy(lower_in, lower_ref, sem.at[1]),
    ]
    for copy in copies:
        copy.start()
    for copy in copies:
        copy.wait()


def solution(mesh):
    sizes = tuple(mesh.shape[name] for name in ("tx", "ty", "ang"))
    n_ang = sizes[2]

    def on_device(projections, view_angles, tilt, offsets, extents, feather):
        _, _, views, rows, width = projections.shape
        band = rows // 2
        g = jnp.asarray(forward_half_table())
        t = jnp.asarray(inverse_half_tables(views * n_ang))
        vmem = pl.BlockSpec(memory_space=pltpu.VMEM)
        hbm = pl.BlockSpec(memory_space=pltpu.HBM)
        f32 = jnp.float32
        results = pl.pallas_call(
            functools.partial(kernel, sizes, views),
            out_shape=[pltpu.VMEM((band, width), f32)] * 2,
            in_specs=[hbm] * 8,
            out_specs=[vmem, vmem],
            scratch_shapes=[
                pltpu.VMEM((1, views), f32),
                pltpu.SMEM((1, 1), f32),
                pltpu.SMEM((1, 1), jnp.int32),
                pltpu.SMEM((1, 1), jnp.int32),
                pltpu.SMEM((1, 2, band), jnp.int32),
                pltpu.VMEM((views, rows, width), jnp.bfloat16),
                pltpu.VMEM((F, width), jnp.bfloat16),
                pltpu.VMEM((2, F, F), jnp.bfloat16),
                pltpu.VMEM((2 * views * rows, width), f32),
                pltpu.VMEM((views * rows, F), f32),
                pltpu.VMEM((views * rows, F), f32),
                pltpu.VMEM((4, views, F), f32),
                pltpu.VMEM((4, views, F), f32),
                pltpu.VMEM((views, BLOCK), f32),
                pltpu.VMEM((2, n_ang * rows, F), f32),
                pltpu.VMEM((n_ang, rows, F), f32),
                pltpu.VMEM((n_ang, rows, F), f32),
                *[pltpu.VMEM((n_ang // 2, rows, F), f32)] * 4,
                *[pltpu.VMEM((n_ang // 4, rows, F), f32)] * 4,
                *[pltpu.VMEM((rows, F), f32)] * 2,
                *[pltpu.VMEM((n_ang // 2, rows, F), f32)] * 2,
                *[pltpu.VMEM((rows, F), f32)] * 2,
                pltpu.VMEM((n_ang // 2, rows, F), f32),
                pltpu.VMEM((n_ang // 2, rows, BLOCK), f32),
                pltpu.VMEM((rows, F), f32),
                pltpu.VMEM((rows, BLOCK), f32),
                pltpu.SemaphoreType.DMA((3,)),
                pltpu.SemaphoreType.DMA((5,)),
                pltpu.SemaphoreType.DMA((32,)),
                pltpu.SemaphoreType.DMA((32,)),
                pltpu.SemaphoreType.REGULAR,
            ],
            compiler_params=pltpu.CompilerParams(collective_id=0, has_side_effects=True),
        )(projections[0, 0], g, t, view_angles[0], tilt, offsets, extents, feather[0])
        anywhere = pl.BlockSpec(memory_space=pl.ANY)
        seams, lower = pl.pallas_call(
            hand_over,
            out_shape=[jax.ShapeDtypeStruct((band, width), f32)] * 2,
            in_specs=[anywhere] * 2,
            out_specs=[anywhere] * 2,
            scratch_shapes=[pltpu.SemaphoreType.DMA((2,))],
        )(*(pltpu.with_memory_space_constraint(r, pltpu.VMEM) for r in results))
        return (seams[None, None, None], lower[None, None, None])

    in_specs = (
        P("tx", "ty", "ang", None, None),
        P("tx", "ty", "ang"),
        P("tx", "ty"),
        P("tx", "ty"),
        P("tx", "ty"),
        P("tx", "ty", None, None),
    )
    out_specs = (P("tx", "ty", "ang", None, None), P("tx", "ty", "ang", None, None))
    return jax.shard_map(
        on_device, mesh=mesh, in_specs=in_specs, out_specs=out_specs, check_vma=False
    )
```

```python
import functools
import math

import jax
import jax.numpy as jnp
import ml_dtypes
import numpy as np
from jax import lax
from jax.experimental import pallas as pl
from jax.experimental.pallas import tpu as pltpu
from jax.sharding import PartitionSpec as P

MESH = pl.DeviceIdType.MESH
PITCH = 16.0
U = 1024
F = U // 2
BLOCK = 128
DXMAX = 128

SIN_HALF = (3.1415926401307073, -5.167710083507923, 2.5500775232148563, -0.5982912856211671, 0.07765766030589402)
COS_HALF = (0.9999999532476085, -4.934792830619664, 4.058411352862771, -1.3318765680813944, 0.21968961109803095)


def forward_half_tables():
    column = np.arange(U // 2)[:, None]
    halves = []
    for start in (0, 1):
        freq = np.arange(start, F, 2)[None, :]
        turn = (column * freq % U) * (2.0 * math.pi / U)
        filt = (freq + 0.5) / F / math.sqrt(U)
        halves.append(np.concatenate([np.cos(turn) * filt, -np.sin(turn) * filt], axis=1))
    return np.stack(halves).astype(np.float32).astype(ml_dtypes.bfloat16)


def inverse_half_tables(views):
    scale = math.sqrt(2.0 / U) / math.sqrt(views)
    place = np.arange(U // 2)[None, :]
    halves = []
    for start in (0, 1):
        freq = np.arange(start, F, 2)[:, None]
        turn = (freq * place % U) * (2.0 * math.pi / U)
        halves.append(np.concatenate([np.cos(turn), -np.sin(turn)], axis=0) * scale)
    return np.stack(halves).astype(np.float32).astype(ml_dtypes.bfloat16)


def horner(z, coefficients):
    total = jnp.full_like(z, coefficients[-1])
    for c in coefficients[-2::-1]:
        total = total * z + c
    return total


def cos_sin_turns(t):
    r = t - jnp.round(t)
    z = r * r
    s = r * horner(z, SIN_HALF)
    c = horner(z, COS_HALF)
    return 1.0 - 2.0 * (s * s), 2.0 * (s * c)


def cos_sin_angle(theta):
    h = theta * 0.5
    z = h * h
    s = h * horner(z, [(-1.0) ** n / math.factorial(2 * n + 1) for n in range(8)])
    c = horner(z, [(-1.0) ** n / math.factorial(2 * n) for n in range(9)])
    return 1.0 - 2.0 * (s * s), 2.0 * (s * c)


def kernel(
    sizes, views,
    x_hbm, g_hbm, t_hbm, angles_hbm, tilt_hbm, offset_hbm, extent_hbm, feather_hbm,
    seams_ref, lower_ref,
    angles_ref, tilt_ref, offset_ref, extent_ref, feather_ref, x_buf, g_buf, t_buf, spec_buf, ycos, ysin, zcos, zsin, col_buf, q_buf,
    bot, top, bot_near, top_near, bot_pair, top_pair, bot_mid, top_mid, bot_four, top_four, bot_last, top_last, bot_far, top_far,
    bot_sum, top_sum, cross_in, corners_in, below_buf, corner_sum,
    load_sem, small_sem, send_sem, recv_sem, ready_sem,
):
    n_tx, n_ty, n_ang = sizes
    tx, ty, me = lax.axis_index("tx"), lax.axis_index("ty"), lax.axis_index("ang")
    tx_prev, tx_next = lax.rem(tx + n_tx - 1, n_tx), lax.rem(tx + 1, n_tx)
    early, late = lax.rem(ty, 2) == 0, lax.rem(ty, 2) == 1
    has_above = ty > 0
    late_sends = late & (ty < n_ty - 1)

    small = [
        pltpu.make_async_copy(src, dst, small_sem.at[n])
        for n, (src, dst) in enumerate((
            (angles_hbm, angles_ref), (tilt_hbm, tilt_ref), (offset_hbm, offset_ref),
            (extent_hbm, extent_ref), (feather_hbm, feather_ref),
        ))
    ]
    for copy in small:
        copy.start()
    load_x = pltpu.make_async_copy(x_hbm, x_buf, load_sem.at[0])
    load_g = [pltpu.make_async_copy(g_hbm.at[part], g_buf.at[part], load_sem.at[1 + part]) for part in range(2)]
    load_t = [pltpu.make_async_copy(t_hbm.at[part], t_buf.at[part], load_sem.at[3 + part]) for part in range(2)]
    load_x.start()
    for load in load_g + load_t:
        load.start()

    barrier = pltpu.get_barrier_semaphore()

    def greet(*device):
        pl.semaphore_signal(barrier, inc=1, device_id=device, device_id_type=MESH)

    bits = [lax.rem(me, 2), lax.rem(me // 2, 2), me // 4]
    partners = [me + step * (1 - 2 * bit) for step, bit in zip((1, 2, 4), bits)]
    half, parity = me // 2, bits[0]
    n_pair = n_ang // 2
    greet(tx, ty, partners[0])
    greet(tx, ty, partners[1])
    greet(tx, ty, partners[2])

    @pl.when(late)
    def _():
        greet(tx_next, ty, me)

    @pl.when(early)
    def _():
        greet(tx, ty, partners[1] + partners[2] - me)
        greet(tx, ty + 1, me)

    @pl.when(early & has_above)
    def _():
        for i in range(n_pair):
            greet(tx, ty - 1, 2 * i + parity)
            greet(tx_next, ty - 1, 2 * i + parity)

    small[0].wait()
    small[1].wait()
    lean = tilt_ref[0, 0]
    rows_i = lax.broadcasted_iota(jnp.int32, (views, views), 0)
    cols_i = lax.broadcasted_iota(jnp.int32, (views, views), 1)
    spread = jnp.where(rows_i == cols_i, jnp.broadcast_to(angles_ref[...], (views, views)), 0.0)
    theta = jnp.broadcast_to(jnp.sum(spread, axis=1, keepdims=True), (views, BLOCK))
    cth, sth = cos_sin_angle(theta)
    col_buf[...] = sth * lean
    zcoef = cth * (lean * (0.5 * PITCH / U))
    band = 4
    sub = lax.broadcasted_iota(jnp.int32, (8, BLOCK), 0)
    ycoord = jnp.where(sub < band, sub, sub + (U - 2 * band)) - U // 2
    ycoef = ycoord.astype(jnp.float32) * (1.0 / U)
    lane = lax.broadcasted_iota(jnp.int32, (8, BLOCK), 1)
    for i in range(4):
        at = slice(BLOCK * i, BLOCK * (i + 1))
        freq8 = (lane * 2 + (2 * BLOCK * (i % 2) + i // 2)).astype(jnp.float32)
        freq = jnp.concatenate([freq8] * (views // 8), axis=0)
        c1, s1 = cos_sin_turns(zcoef * freq)
        c2, s2 = 1.0 - 2.0 * (s1 * s1), 2.0 * (s1 * c1)
        c, s = c1, s1
        for j in range(4):
            zcos[j, :, at] = c
            zsin[j, :, at] = s
            if j < 3:
                c, s = c * c2 - s * s2, c * s2 + s * c2
        for k in range(views):
            slope = jnp.broadcast_to(col_buf[k : k + 1, :], (8, BLOCK)) * ycoef
            c, s = cos_sin_turns(slope * freq8)
            ycos[8 * k : 8 * k + 8, at] = c
            ysin[8 * k : 8 * k + 8, at] = s

    load_x.wait()
    rows = views * 8
    left = x_buf[:, :, : U // 2].reshape(rows, U // 2)
    right = x_buf[:, :, U // 2 :].reshape(rows, U // 2)
    halves_of_x = jnp.concatenate([left, right], axis=0)
    for part in range(2):
        load_g[part].wait()
        spec_buf[part] = jnp.dot(halves_of_x, g_buf[part], preferred_element_type=jnp.float32)

    for i in range(4):
        at = slice(BLOCK * i, BLOCK * (i + 1))
        part, col = i // 2, BLOCK * (i % 2)
        spec = spec_buf.at[part]
        at_re, at_im = slice(col, col + BLOCK), slice(F // 2 + col, F // 2 + col + BLOCK)
        acc = [[jnp.zeros((8, BLOCK), jnp.float32) for _ in range(4)] for _ in range(4)]
        for k in range(views):
            here, there = slice(8 * k, 8 * k + 8), slice(rows + 8 * k, rows + 8 * k + 8)
            if i < 2:
                s_re = spec[here, at_re] + spec[there, at_re]
                s_im = spec[here, at_im] + spec[there, at_im]
            else:
                s_re = spec[here, at_re] - spec[there, at_re]
                s_im = spec[here, at_im] - spec[there, at_im]
            yc, ys = ycos[here, at], ysin[here, at]
            p_re = s_re * yc - s_im * ys
            p_im = s_re * ys + s_im * yc
            for j in range(4):
                c = jnp.broadcast_to(zcos[j, k : k + 1, at], (8, BLOCK))
                s = jnp.broadcast_to(zsin[j, k : k + 1, at], (8, BLOCK))
                acc[j][0] += c * p_re
                acc[j][1] += c * p_im
                acc[j][2] += s * p_re
                acc[j][3] += s * p_im
        for j in range(4):
            c_re, c_im, s_re, s_im = acc[j]
            for plane, re, im in (
                (4 + j, c_re - s_im, c_im + s_re),
                (3 - j, c_re + s_im, c_im - s_re),
            ):
                at_row = slice(8 * plane, 8 * plane + 8)
                q_buf[part, at_row, col : col + BLOCK] = re
                q_buf[part, at_row, F // 2 + col : F // 2 + col + BLOCK] = im

    halves = []
    for part in range(2):
        load_t[part].wait()
        q = q_buf[part]
        high = q.astype(jnp.bfloat16)
        low = (q - high.astype(jnp.float32)).astype(jnp.bfloat16)
        both = jnp.dot(
            jnp.concatenate([high, low], axis=0), t_buf[part], preferred_element_type=jnp.float32
        )
        halves.append(both[: 8 * 8] + both[8 * 8 :])
    first, second = halves[0] + halves[1], halves[0] - halves[1]
    sub_wide = lax.broadcasted_iota(jnp.int32, (8, F), 0)
    upper = sub_wide < band
    for plane in range(8):
        a, b = first[8 * plane : 8 * plane + 8], second[8 * plane : 8 * plane + 8]
        bot[plane] = jnp.where(upper, pltpu.roll(a, band, 0), b)

    greeted = n_pair + late.astype(jnp.int32)
    pl.semaphore_wait(barrier, greeted + 2 * n_pair * late_sends.astype(jnp.int32))

    bands = (
        (0, bot, bot_near, bot_pair, bot_mid, bot_four, bot_last),
        (1, top, top_near, top_pair, top_mid, top_four, top_last),
    )
    far_slots = (bot_far, top_far)

    def swap(src, dst, sem, partner):
        return pltpu.make_async_remote_copy(
            src_ref=src, dst_ref=dst, send_sem=send_sem.at[sem], recv_sem=recv_sem.at[sem],
            device_id=(tx, ty, partner), device_id_type=MESH,
        )

    def near(band_of, i):
        which, mine, landed = band_of[:3]
        return swap(mine.at[2 * i + 1 - parity], landed.at[i], 7 * which + i, partners[0])

    def mid(band_of, j):
        which, pair, landed = band_of[0], band_of[3], band_of[4]
        return swap(pair.at[2 * j + 1 - bits[1]], landed.at[j], 7 * which + 4 + j, partners[1])

    def last(band_of):
        which, four, landed = band_of[0], band_of[5], band_of[6]
        return swap(four.at[1 - bits[2]], landed, 7 * which + 6, partners[2])

    def paired(band_of, i):
        _, mine, landed, pair = band_of[:4]
        near(band_of, i).wait_recv()
        pair[i] = mine[2 * i + parity] + landed[i]

    def four(band_of, j):
        _, _, _, pair, landed, fours, _ = band_of
        mid(band_of, j).wait_recv()
        fours[j] = pair[2 * j + bits[1]] + landed[j]

    def send_last(band_of):
        four(band_of, 1 - bits[2])
        last(band_of).start()

    def gathered(band_of):
        fours, landed = band_of[5:]
        four(band_of, bits[2])
        last(band_of).wait_recv()
        return fours[bits[2]] + landed[...]

    def far(band_of, i, origin):
        which, pair = band_of[0], band_of[3]
        return pltpu.make_async_remote_copy(
            src_ref=pair.at[i], dst_ref=far_slots[which].at[origin],
            send_sem=send_sem.at[24 + 4 * which + i], recv_sem=recv_sem.at[24 + 4 * which + origin],
            device_id=(tx, ty, 2 * i + parity), device_id_type=MESH,
        )

    def send_far(band_of, i):
        @pl.when(i != half)
        def _():
            far(band_of, i, half).start()

    def gathered_far(band_of):
        total = band_of[3][half]
        for d in range(1, n_pair):
            origin = lax.rem(half + d, n_pair)
            far(band_of, half, origin).wait_recv()
            total += far_slots[band_of[0]][origin]
        return total

    def straight(i, origin):
        return pltpu.make_async_remote_copy(
            src_ref=bot_pair.at[i], dst_ref=cross_in.at[origin],
            send_sem=send_sem.at[14 + i], recv_sem=recv_sem.at[14 + origin],
            device_id=(tx, ty + 1, 2 * i + parity), device_id_type=MESH,
        )

    def slanted(i, origin):
        return pltpu.make_async_remote_copy(
            src_ref=bot_pair.at[i, pl.ds(0, 4), pl.ds(0, BLOCK)], dst_ref=corners_in.at[origin, pl.ds(0, 4)],
            send_sem=send_sem.at[18 + i], recv_sem=recv_sem.at[18 + origin],
            device_id=(tx_prev, ty + 1, 2 * i + parity), device_id_type=MESH,
        )

    down = pltpu.make_async_remote_copy(
        src_ref=bot_sum, dst_ref=below_buf, send_sem=send_sem.at[22], recv_sem=recv_sem.at[22],
        device_id=(tx, ty + 1, me), device_id_type=MESH,
    )
    across = pltpu.make_async_remote_copy(
        src_ref=below_buf.at[:, pl.ds(0, BLOCK)], dst_ref=corners_in.at[0],
        send_sem=send_sem.at[23], recv_sem=recv_sem.at[23],
        device_id=(tx_prev, ty, me), device_id_type=MESH,
    )

    @pl.when(late)
    def _():
        pl.semaphore_signal(ready_sem, inc=1, device_id=(tx, ty - 1, me), device_id_type=MESH)

    lower_part, upper_part = bands
    held = [late & (parity == 0) & (half < 2), late & (parity == 0) & (half >= 2)]
    plans = ({2: (0, 1, 2, 3)}, {1: (1, 2), 2: (3,)})
    for i in range(n_pair):
        near(lower_part, jnp.where(early, n_pair - 1 - i, i)).start()

    for plane in range(8):
        a, b = first[8 * plane : 8 * plane + 8], second[8 * plane : 8 * plane + 8]
        top[plane] = jnp.where(upper, a, pltpu.roll(b, band, 0))

    for i in range(n_pair):
        @pl.when((late & (parity == 1)) | (held[1] & (i < 1)))
        def _():
            near(upper_part, i).start()

    @pl.when(late)
    def _():
        for i in range(n_pair):
            for group, plan in zip(held, plans):
                @pl.when(group)
                def _(plan=plan):
                    for k in plan.get(i, ()):
                        near(upper_part, k).start()

            paired(lower_part, i)

            @pl.when(late_sends)
            def _():
                slanted(i, half).start()
                straight(i, half).start()

        for j in range(n_pair // 2):
            mid(lower_part, j).start()
        for i in range(n_pair):
            paired(upper_part, i)

            @pl.when(bits[1] == 1 - i % 2)
            def _():
                mid(upper_part, i // 2).start()

        send_last(lower_part)
        send_last(upper_part)
        bot_sum[...] = gathered(lower_part)
        top_sum[...] = gathered(upper_part)

    @pl.when(early)
    def _():
        for i in reversed(range(n_pair)):
            paired(lower_part, i)
            send_far(lower_part, i)
        for i in range(n_pair):
            near(upper_part, i).start()
        for i in range(n_pair):
            paired(upper_part, i)
            send_far(upper_part, i)
        bot_sum[...] = gathered_far(lower_part)
        pl.semaphore_wait(ready_sem, 1)
        down.start()
        top_sum[...] = gathered_far(upper_part)

    bottom = bot_sum[...]
    lower_ref[:, :F] = bottom[:band]
    lower_ref[:, F:] = pltpu.roll(bottom, band, 0)[:band]

    @pl.when(late)
    def _():
        down.wait_recv()

    @pl.when(early & has_above)
    def _():
        for origin in range(n_pair):
            slanted(half, origin).wait_recv()
            straight(half, origin).wait_recv()
        below_buf[...] = (cross_in[0] + cross_in[1]) + (cross_in[2] + cross_in[3])
        corner_sum[...] = (corners_in[0] + corners_in[1]) + (corners_in[2] + corners_in[3])

    @pl.when(ty == 0)
    def _():
        below_buf[...] = jnp.zeros_like(below_buf)
        corner_sum[...] = jnp.zeros_like(corner_sum)

    @pl.when(late)
    def _():
        across.start()

    for copy in small[2:]:
        copy.wait()
    row = sub % band
    own = jnp.zeros((8, BLOCK), jnp.float32)
    other = jnp.zeros((8, BLOCK), jnp.float32)
    seen = (ty > 0).astype(jnp.int32)
    for r in range(band):
        a = feather_ref[0, 0, r].astype(jnp.float32)
        b = (feather_ref[0, 1, r] * (r < extent_ref[0, 0]).astype(jnp.int32) * seen).astype(jnp.float32)
        own = jnp.where(row == r, a, own)
        other = jnp.where(row == r, b, other)
    total = jnp.maximum(own + other, 1.0)
    own, other = own / total, other / total
    shift = offset_ref[0, 0]
    turn_by = (BLOCK - shift) & (BLOCK - 1)

    @pl.when(late)
    def _():
        across.wait_recv()
        corner_sum[...] = corners_in[0]

    own_top = top_sum[...]
    below = below_buf[...]
    corner = jnp.where(tx < n_tx - 1, corner_sum[...], 0.0)
    tail = pltpu.roll(jnp.where(sub < band, corner, below[:, :BLOCK]), band, 0)
    pieces = [below[:, BLOCK * i : BLOCK * (i + 1)] for i in range(4)] + [tail]
    turned = [pltpu.roll(piece, turn_by, 1) for piece in pieces]
    for i in range(4):
        aligned = jnp.where(lane < BLOCK - shift, turned[i], turned[i + 1])
        seam = own * own_top[:, BLOCK * i : BLOCK * (i + 1)] + other * aligned
        seams_ref[:, BLOCK * i : BLOCK * (i + 1)] = seam[:band]
        seams_ref[:, F + BLOCK * i : F + BLOCK * (i + 1)] = pltpu.roll(seam, band, 0)[:band]

    for band_of in bands:
        for i in range(n_pair):
            near(band_of, i).wait_send()

        @pl.when(late)
        def _():
            for j in range(n_pair // 2):
                mid(band_of, j).wait_send()
            last(band_of).wait_send()

        @pl.when(early)
        def _():
            for d in range(1, n_pair):
                far(band_of, lax.rem(half + d, n_pair), half).wait_send()

    @pl.when(late_sends)
    def _():
        for i in range(n_pair):
            slanted(i, half).wait_send()
            straight(i, half).wait_send()

    @pl.when(early)
    def _():
        down.wait_send()

    @pl.when(late)
    def _():
        across.wait_send()


def hand_over(seams_in, lower_in, seams_ref, lower_ref, sem):
    copies = [
        pltpu.make_async_copy(seams_in, seams_ref, sem.at[0]),
        pltpu.make_async_copy(lower_in, lower_ref, sem.at[1]),
    ]
    for copy in copies:
        copy.start()
    for copy in copies:
        copy.wait()


def solution(mesh):
    sizes = tuple(mesh.shape[name] for name in ("tx", "ty", "ang"))
    n_ang = sizes[2]

    def on_device(projections, view_angles, tilt, offsets, extents, feather):
        _, _, views, rows, width = projections.shape
        band = rows // 2
        g = jnp.asarray(forward_half_tables())
        t = jnp.asarray(inverse_half_tables(views * n_ang))
        vmem = pl.BlockSpec(memory_space=pltpu.VMEM)
        hbm = pl.BlockSpec(memory_space=pltpu.HBM)
        f32 = jnp.float32
        results = pl.pallas_call(
            functools.partial(kernel, sizes, views),
            out_shape=[pltpu.VMEM((band, width), f32)] * 2,
            in_specs=[hbm] * 8,
            out_specs=[vmem, vmem],
            scratch_shapes=[
                pltpu.VMEM((1, views), f32),
                pltpu.SMEM((1, 1), f32),
                pltpu.SMEM((1, 1), jnp.int32),
                pltpu.SMEM((1, 1), jnp.int32),
                pltpu.SMEM((1, 2, band), jnp.int32),
                pltpu.VMEM((views, rows, width), jnp.bfloat16),
                pltpu.VMEM((2, F, F), jnp.bfloat16),
                pltpu.VMEM((2, F, F), jnp.bfloat16),
                pltpu.VMEM((2, 2 * views * rows, F), f32),
                pltpu.VMEM((views * rows, F), f32),
                pltpu.VMEM((views * rows, F), f32),
                pltpu.VMEM((4, views, F), f32),
                pltpu.VMEM((4, views, F), f32),
                pltpu.VMEM((views, BLOCK), f32),
                pltpu.VMEM((2, n_ang * rows, F), f32),
                pltpu.VMEM((n_ang, rows, F), f32),
                pltpu.VMEM((n_ang, rows, F), f32),
                *[pltpu.VMEM((n_ang // 2, rows, F), f32)] * 4,
                *[pltpu.VMEM((n_ang // 4, rows, F), f32)] * 4,
                *[pltpu.VMEM((rows, F), f32)] * 2,
                *[pltpu.VMEM((n_ang // 2, rows, F), f32)] * 2,
                *[pltpu.VMEM((rows, F), f32)] * 2,
                pltpu.VMEM((n_ang // 2, rows, F), f32),
                pltpu.VMEM((n_ang // 2, rows, BLOCK), f32),
                pltpu.VMEM((rows, F), f32),
                pltpu.VMEM((rows, BLOCK), f32),
                pltpu.SemaphoreType.DMA((5,)),
                pltpu.SemaphoreType.DMA((5,)),
                pltpu.SemaphoreType.DMA((32,)),
                pltpu.SemaphoreType.DMA((32,)),
                pltpu.SemaphoreType.REGULAR,
            ],
            compiler_params=pltpu.CompilerParams(collective_id=0, has_side_effects=True),
        )(projections[0, 0], g, t, view_angles[0], tilt, offsets, extents, feather[0])
        anywhere = pl.BlockSpec(memory_space=pl.ANY)
        seams, lower = pl.pallas_call(
            hand_over,
            out_shape=[jax.ShapeDtypeStruct((band, width), f32)] * 2,
            in_specs=[anywhere] * 2,
            out_specs=[anywhere] * 2,
            scratch_shapes=[pltpu.SemaphoreType.DMA((2,))],
        )(*(pltpu.with_memory_space_constraint(r, pltpu.VMEM) for r in results))
        return (seams[None, None, None], lower[None, None, None])

    in_specs = (
        P("tx", "ty", "ang", None, None),
        P("tx", "ty", "ang"),
        P("tx", "ty"),
        P("tx", "ty"),
        P("tx", "ty"),
        P("tx", "ty", None, None),
    )
    out_specs = (P("tx", "ty", "ang", None, None), P("tx", "ty", "ang", None, None))
    return jax.shard_map(
        on_device, mesh=mesh, in_specs=in_specs, out_specs=out_specs, check_vma=False
    )
```
